32 devices in a mesh: groups: 2 (over y), seq: 4 (over z), batch: 2 (over x), head: 2 (over core).
Axes of the slice: x: 2, y: 2, z: 4, core: 2. Of those that a mesh axis runs over, the one named last changes fastest.
Arguments:
- x_inner: bfloat16 [4, 2048, 3072], P(('groups', 'batch'), 'seq', 'head'), parts along dimension 0, may hold values from -6 to 6
- gating_branch_values: bfloat16 [4, 2048, 3072], P(('groups', 'batch'), 'seq', 'head'), parts along dimension 0, may hold values from -6 to 6
- b_proj: bfloat16 [4, 2048, 128], P(('groups', 'batch'), 'seq'), parts along dimension 0, may hold values from -2 to 2
- c_proj: bfloat16 [4, 2048, 128], P(('groups', 'batch'), 'seq'), parts along dimension 0, may hold values from -2 to 2
- unbiased_step_size: float32 [4, 2048, 48], P(('groups', 'batch'), 'seq', 'head'), parts along dimension 0, may hold values from -3 to 10
- record_lengths: int32 [4, 2], P(('groups', 'batch')), parts along dimension 0, may hold values from 1 to 1536, 2048 in all within a row
- dt_bias: float32 [48], P('head'), may hold values from -9 to -3
- a_log: float32 [48], P('head'), may hold values from -0.5 to 0.5
- d_skip: float32 [48], P('head'), may hold values from 0.5 to 1.5
- norm_gain: float32 [3072], P('head'), may hold values from 0.5 to 1.5
- out_grad: bfloat16 [4, 2048, 3072], P(('groups', 'batch'), 'seq', 'head'), parts along dimension 0, may hold values from -6 to 6
Outputs:
- normed: bfloat16 [4, 2048, 3072], P(('groups', 'batch'), 'seq', 'head'), parts along dimension 0
- x_grad: bfloat16 [4, 2048, 3072], P(('groups', 'batch'), 'seq', 'head'), parts along dimension 0
- z_grad: bfloat16 [4, 2048, 3072], P(('groups', 'batch'), 'seq', 'head'), parts along dimension 0
- input_matrix_gradient: float32 [4, 2048, 128], P(('groups', 'batch'), 'seq'), parts along dimension 0
- c_grad: float32 [4, 2048, 128], P(('groups', 'batch'), 'seq'), parts along dimension 0
- dt_grad: float32 [4, 2048, 48], P(('groups', 'batch'), 'seq', 'head'), parts along dimension 0
- bias_grad: float32 [96], P(('groups', 'head')), parts along dimension 0
- alog_grad: float32 [96], P(('groups', 'head')), parts along dimension 0
- residual_factor_cotangent: float32 [96], P(('groups', 'head')), parts along dimension 0
- gain_grad: float32 [6144], P(('groups', 'head')), parts along dimension 0
The draws below stay inside these ranges and needn't reach their ends.
There are 2 independent parts, one for each index of `groups`. The reference program is written for one: setup_inputs(seed, part) draws one part's arguments, and reference() takes and returns one part's arrays. A program takes and returns all parts, laid end to end along the dimension named above; an argument that names none is the same for every part. Nothing has to cross between parts.
Inputs may be any that keep to these rules, and one draw needn't show every extreme that they name: `record_lengths`: each row's lengths sum to 2048; no record of a row has more than 1536 positions.
All inputs are finite; a program needn't handle non-finite values.
Results may differ from the reference program's by a relative error of at most 0.001.
Values sent between devices are 32-bit elements; how exact they have to be, the bound alone decides.
No kernel may reach another device: no remote copies, remote signals or barrier semaphores. Data moves between devices by JAX's collectives and lax.ppermute only.
A program may use at most 192 MiB of HBM per device.

```python
import math
from functools import partial
import jax
import jax.numpy as jnp
import numpy as np
from jax import lax

STATE = 128
HEADDIM = 64
SPAN = 256
HEADS = 48
RECORDS = 2
SEQ_LEN = 2048
ROWS = 2
INNER = 3072
LONGEST = 1536


def draw_unbiased_step_size(key, part):
    noise_key, spot_key = jax.random.split(key)
    shape = (ROWS, SEQ_LEN, HEADS)
    starting_shift_amount = jnp.clip(0.5 * jax.random.normal(noise_key, shape, jnp.float32), -3.0, 3.0)
    reading_spots = jax.random.randint(spot_key, (ROWS, 4), 0, SEQ_LEN)
    element_places = jnp.arange(SEQ_LEN)
    impulse_span_range = jnp.any(element_places[None, :, None] == reading_spots[:, None, :], axis=-1).astype(jnp.float32)
    return starting_shift_amount + 7.0 * impulse_span_range[:, :, None]


def draw_dt_bias(key, part):
    values = jax.random.uniform(key, (HEADS,), jnp.float32, -7.5, -3.0)
    return values


def block_scale(rng, extent, cuts, least, largest):
    def one(dim, shards_of):
        steps = jax.random.uniform(jax.random.fold_in(jax.random.fold_in(rng, 6), dim), (shards_of,), jnp.float32, least / len(cuts), largest / len(cuts))
        return jnp.repeat(jnp.exp(steps), extent[dim] // shards_of).reshape((-1,) + (1,) * (len(extent) - dim - 1))

    level = one(*cuts[0])
    for cut in cuts[1:]:
        level = level * one(*cut)
    return level


def profile(amount, total, most, slope):
    loads = [(1 << 20) // math.isqrt(standing ** slope) + 1 for standing in range(2, amount + 1)]
    surplus, counts = total - most - (amount - 1), [1] * (amount - 1)
    while surplus > 0:
        movable = [i for i in range(amount - 1) if counts[i] < most]
        pool, left = sum([loads[i] for i in movable]), surplus
        for i in movable:
            more = min(most - counts[i], max(1, left * loads[i] // pool), surplus)
            counts[i] = counts[i] + more
            surplus = surplus - more
    return np.array([most] + counts)


def uneven(rng, number_of, total, limit, skew):
    if number_of == 2:
        one = jax.random.randint(rng, (), max(1, total - limit), min(limit, total - 1) + 1)
        return jnp.stack([one, total - one])
    lengths = jnp.asarray(profile(number_of, total, limit, skew), jnp.int32)
    couples = (number_of - 1) // 2
    donor, receiver = lengths[1:1 + 2 * couples:2], lengths[2:2 + 2 * couples:2]
    margin = jnp.minimum(donor - 1, limit - receiver)
    passed = jax.random.randint(jax.random.fold_in(rng, 1), (couples,), 0, 1 << 20) % (margin + 1)
    lengths = lengths.at[1:1 + 2 * couples:2].set(donor - passed).at[2:2 + 2 * couples:2].set(receiver + passed)
    return lengths[jax.random.permutation(jax.random.fold_in(rng, 2), number_of)]


def gaussian(own_key, dims, spread, most, shards=(), kind=jnp.bfloat16):
    entries = spread * jax.random.normal(own_key, dims, jnp.float32)
    if shards:
        entries = entries * block_scale(own_key, dims, shards, -0.22, 0.18)
    return jnp.clip(entries, -most, most).astype(kind)


def setup_inputs(seed: int = 0, part: int = 0) -> dict:
    seeds = jax.random.split(jax.random.key(seed), 12)
    part_keys = jax.random.split(jax.random.fold_in(seeds[11], part), 12)
    return {
        "x_inner": gaussian(part_keys[0], (ROWS, SEQ_LEN, INNER), 1.0, 6.0, ((0, 2), (1, 4), (2, 2))),
        "gating_branch_values": gaussian(part_keys[1], (ROWS, SEQ_LEN, INNER), 1.0, 6.0, ((0, 2), (1, 4), (2, 2))),
        "b_proj": gaussian(part_keys[2], (ROWS, SEQ_LEN, STATE), 0.3, 2.0, ((0, 2), (1, 4))),
        "c_proj": gaussian(part_keys[3], (ROWS, SEQ_LEN, STATE), 0.3, 2.0, ((0, 2), (1, 4))),
        "unbiased_step_size": draw_unbiased_step_size(jax.random.fold_in(jax.random.fold_in(seeds[11], part), 71), part),
        "record_lengths": jax.vmap(lambda own: uneven(own, RECORDS, SEQ_LEN, LONGEST, 2))(jax.random.split(part_keys[5], ROWS)).reshape((ROWS, RECORDS)).astype(jnp.int32),
        "dt_bias": draw_dt_bias(jax.random.fold_in(seeds[11], 71), part),
        "a_log": jnp.clip(jax.random.uniform(seeds[7], (HEADS,), jnp.float32, -0.5, 0.5) * block_scale(seeds[7], (HEADS,), ((0, 2),), -0.4, 0.0), -0.5, 0.5),
        "d_skip": jnp.clip(0.5 + 1.0 * jax.random.uniform(seeds[8], (HEADS,), jnp.float32) ** block_scale(seeds[8], (HEADS,), ((0, 2),), -0.2, 0.2), 0.5, 1.5),
        "norm_gain": jnp.clip(1.0 + 0.1 * jax.random.normal(seeds[9], (INNER,), jnp.float32), 0.5, 1.5),
        "out_grad": gaussian(part_keys[10], (ROWS, SEQ_LEN, INNER), 1.0, 6.0, ((0, 2), (1, 4), (2, 2))),
    }


highest = lax.Precision.HIGHEST
epsilon = 1e-05

def record_ids(record_lengths, element_places):
    starts = jnp.cumsum(record_lengths, axis=1) - record_lengths
    return lax.optimization_barrier(jnp.sum((starts[:, None, :] <= element_places[None, :, None]).astype(jnp.int32), axis=2)).astype(jnp.int32)

def decay_terms(raw_step, segment, prior_value, dt_bias, a_log):
    step_size = jax.nn.softplus(raw_step + dt_bias)
    cumul = jnp.cumsum(step_size * -jnp.exp(a_log), axis=0).T
    closing = segment[-1]
    inflow = jnp.exp(cumul) * (segment == prior_value).astype(jnp.float32)
    decay = jnp.exp(cumul[:, -1]) * (closing == prior_value).astype(jnp.float32)
    tail_weight = jnp.exp(cumul[:, -1:] - cumul) * (segment == closing).astype(jnp.float32)
    return (step_size, cumul, inflow, decay, tail_weight)

def block_step(state, block, dt_bias, a_log, d_skip):
    x_block, raw_step, b_block, c_block, segment, prior_value = block
    x_float = x_block.astype(jnp.float32)
    step_size, cumul, inflow, decay, tail_weight = decay_terms(raw_step, segment, prior_value, dt_bias, a_log)
    position = jnp.arange(segment.shape[0])
    same_rec = (segment[:, None] == segment[None, :]) & (position[:, None] >= position[None, :])
    log_gap = jnp.where(same_rec[None], cumul[:, :, None] - cumul[:, None, :], 0.0)
    scores = jnp.dot(c_block, b_block.T, precision=highest)
    mixing = jnp.where(same_rec[None], jnp.exp(log_gap), 0.0) * scores[None]
    rescaled_quantity = x_float * step_size[:, :, None]
    result = jnp.einsum('hij,jhp->ihp', mixing, rescaled_quantity, precision=highest)
    result = result + jnp.einsum('in,hpn->ihp', c_block, state, precision=highest) * inflow.T[:, :, None]
    result = result + d_skip[None, :, None] * x_float
    fresh = jnp.einsum('jhp,jn->hpn', rescaled_quantity * tail_weight.T[:, :, None], b_block, precision=highest)
    return (decay[:, None, None] * state + fresh, result)

def reference(x_inner, gating_branch_values, b_proj, c_proj, unbiased_step_size, record_lengths, dt_bias, a_log, d_skip, norm_gain, out_grad):
    count = SEQ_LEN // SPAN
    element_places = jnp.arange(SEQ_LEN, dtype=jnp.int32)
    segments = record_ids(record_lengths, element_places).reshape(ROWS, count, SPAN)
    prior_value = record_ids(record_lengths, jnp.arange(count, dtype=jnp.int32) * SPAN - 1)
    start_state = jnp.zeros((ROWS, HEADS, HEADDIM, STATE), jnp.float32)

    def forward(x_value, z_value, b_value, c_value, raw_value, step_bias_entry, alog_value, skip_value, gain_value):

        def one_row(x_rows, raw_rows, b_rows, c_rows, state, segment_rows, previous_rows):
            stepper = jax.checkpoint(partial(block_step, dt_bias=step_bias_entry, a_log=alog_value, d_skip=skip_value))
            _, result = lax.scan(stepper, state, (x_rows, raw_rows, b_rows, c_rows, segment_rows, previous_rows))
            return result
        result = jax.vmap(one_row)(x_value.reshape(ROWS, count, SPAN, HEADS, HEADDIM), raw_value.reshape(ROWS, count, SPAN, HEADS), b_value.reshape(ROWS, count, SPAN, STATE), c_value.reshape(ROWS, count, SPAN, STATE), start_state, segments, prior_value)
        result = result.reshape(ROWS, SEQ_LEN, INNER)
        gated = result * jax.nn.silu(z_value.astype(jnp.float32))
        scale = lax.rsqrt(lax.optimization_barrier(jnp.mean(gated * gated, axis=-1, keepdims=True)) + epsilon)
        return gated * scale * gain_value
    normed_full, backward = jax.vjp(forward, x_inner, gating_branch_values, b_proj.astype(jnp.float32), c_proj.astype(jnp.float32), unbiased_step_size, dt_bias, a_log, d_skip, norm_gain)
    grads = backward(out_grad.astype(jnp.float32))
    return (normed_full.astype(jnp.bfloat16), grads[0].astype(jnp.bfloat16), grads[1].astype(jnp.bfloat16), grads[2], grads[3], grads[4], grads[5], grads[6], grads[7], grads[8])
```

```python
from functools import partial

import jax
import jax.numpy as jnp
from jax import lax
from jax.experimental import pallas as pl
from jax.experimental.pallas import tpu as pltpu
from jax.sharding import PartitionSpec as P

STATE = 128
HEADDIM = 64
BLOCK = 128
LANES = 128
GROUP = 32
COLS = 256
CHUNKS = 3
EPSILON = 1e-05
HIGHEST = lax.Precision.HIGHEST
F32 = jnp.float32
BF16 = jnp.bfloat16
VMEM_LIMIT = 56 * 1024 * 1024


def mm(a, b):
    return jnp.dot(a, b, preferred_element_type=F32)


def mm_nt(a, b):
    return lax.dot_general(a, b, (((1,), (1,)), ((), ())), preferred_element_type=F32)


def mm_tn(a, b):
    return lax.dot_general(a, b, (((0,), (0,)), ((), ())), preferred_element_type=F32)


def split(value):
    high = value.astype(BF16)
    return high, (value - high.astype(F32)).astype(BF16)


def iota(shape, axis):
    return lax.broadcasted_iota(jnp.int32, shape, axis)


def pieces(value):
    high = value.astype(BF16).astype(F32)
    rest = value - high
    middle = rest.astype(BF16).astype(F32)
    lane = iota(value.shape, 1)
    chosen = jnp.where(lane < GROUP, high, jnp.where(lane < 2 * GROUP, middle, rest - middle))
    return jnp.where(lane < 3 * GROUP, chosen, 0.0).astype(BF16)


def head_rows(spread, heads):
    tile = (iota((heads, LANES), 1) % GROUP == iota((heads, LANES), 0)).astype(F32)
    return jnp.dot(jnp.broadcast_to(spread, (8, heads)), tile, precision=HIGHEST, preferred_element_type=F32)[0:1]


def count_starts(lengths, position):
    start = jnp.int32(0)
    total = (start <= position).astype(jnp.int32)
    for k in range(1, lengths.shape[0]):
        start = start + lengths[k - 1]
        total = total + (start <= position).astype(jnp.int32)
    return total


def segments(lengths, offset, block):
    base = offset[0] + block * BLOCK
    column = count_starts(lengths, base + iota((BLOCK, 1), 0))
    row = count_starts(lengths, base + iota((1, BLOCK), 1))
    return column, row, count_starts(lengths, base - 1), count_starts(lengths, base + BLOCK - 1)


def prepare_kernel(lengths, offset, raw, bias, alog, x, b, oh, e, total, ends, decs, prefix, step, cum, sig, rows, state, run):
    block = pl.program_id(0)
    heads = raw.shape[1]

    @pl.when(block == 0)
    def _():
        state[...] = jnp.zeros_like(state)
        run[...] = jnp.ones_like(run)

    segment, _, prior, last = segments(lengths, offset, block)
    value = raw[...] + bias[...]
    small = jnp.exp(-jnp.abs(value))
    ratio = small / (2.0 + small)
    square = ratio * ratio
    series = jnp.full_like(square, 1.0 / 19.0)
    for odd in (17, 15, 13, 11, 9, 7, 5, 3, 1):
        series = series * square + 1.0 / odd
    soft = jnp.maximum(value, 0.0) + 2.0 * ratio * series
    inverse = 1.0 / (1.0 + small)
    sigma = jnp.where(value >= 0.0, inverse, small * inverse)
    tile = (iota((heads, LANES), 1) % GROUP == iota((heads, LANES), 0)).astype(F32)
    spread = partial(jnp.dot, precision=HIGHEST, preferred_element_type=F32)
    steps = spread(soft, tile)
    rate = steps * -jnp.exp(head_rows(alog[...], heads))
    lower = (iota((BLOCK, BLOCK), 0) >= iota((BLOCK, BLOCK), 1)).astype(F32)
    cumul = spread(lower, rate)
    step[...] = steps
    cum[...] = cumul
    sig[...] = spread(sigma, tile)
    rows[0] = cumul.T[:GROUP]
    rows[1] = steps.T[:GROUP]
    closing = cumul[BLOCK - 1 : BLOCK, :]
    weight = jnp.exp(closing - cumul) * (segment == last).astype(F32) * steps
    decay = jnp.exp(closing) * (last == prior).astype(F32)
    weights = pieces(weight)
    decays = pieces(jnp.broadcast_to(decay, (8, LANES)))
    width = x.shape[1]
    chunk = e.shape[2]
    for at in range(0, width, COLS):
        col = slice(at, at + COLS)
        high, low = split(x[:, col].astype(F32) * mm(weights, oh[:, col]))
        dec = mm(decays, oh[:, col])[0:1]
        fresh = dec * state[:, col] + (mm_tn(b[...], high) + mm_tn(b[...], low))
        state[:, col] = fresh
        ends[0, :, col] = fresh
        decs[0, :, col] = dec
        product = run[:, col] * dec
        run[:, col] = product
        prefix[0, :, col] = product

    @pl.when(block == pl.num_programs(0) - 1)
    def _():
        for c in range(e.shape[0]):
            e[c] = state[:, c * chunk : (c + 1) * chunk]
            total[c] = run[:, c * chunk : (c + 1) * chunk]


def diagonal_kernel(lengths, offset, cum, rows, x, b, c, out):
    block = pl.program_id(0)
    seg_column, seg_row, _, _ = segments(lengths, offset, block)
    mask = (seg_column == seg_row) & (iota((BLOCK, BLOCK), 0) > iota((BLOCK, BLOCK), 1))
    scores = jnp.where(mask, mm_nt(c[...], b[...]), 0.0)
    left = iota((BLOCK, LANES), 1) < HEADDIM
    for pair in range(x.shape[1] // LANES):
        col = slice(pair * LANES, (pair + 1) * LANES)
        parts = []
        for h in (2 * pair, 2 * pair + 1):
            gap = cum[:, h : h + 1] - rows[0, h : h + 1, :]
            parts.append(split(jnp.exp(jnp.minimum(gap, 0.0)) * scores * rows[1, h : h + 1, :]))
        pair_x = x[:, col]
        zero = jnp.zeros_like(pair_x)
        both = jnp.concatenate([jnp.where(left, pair_x, zero), jnp.where(left, zero, pair_x)], axis=0)
        high = jnp.concatenate([parts[0][0], parts[1][0]], axis=1)
        low = jnp.concatenate([parts[0][1], parts[1][1]], axis=1)
        out[:, col] = mm(high, both) + mm(low, both)


def output_kernel(lengths, offset, sin, ends, prefix, cum, step, x, z, g, b, c, diag, dskip, gain, oh, yp, stats, full, state):
    block = pl.program_id(0)

    @pl.when(block == 0)
    def _():
        state[...] = sin[...]

    segment, _, prior, _ = segments(lengths, offset, block)
    inflow = pieces(jnp.exp(cum[...]) * (segment == prior).astype(F32))
    own = jnp.sum(b[...].astype(F32) * c[...].astype(F32), axis=1, keepdims=True)
    coefficient = pieces(head_rows(dskip[...], dskip.shape[1]) + step[...] * own)
    square = jnp.zeros((BLOCK, COLS), F32)
    cross = jnp.zeros((BLOCK, COLS), F32)
    for at in range(0, x.shape[1], COLS):
        col = slice(at, at + COLS)
        high, low = split(state[:, col])
        carried = mm(c[...], high) + mm(c[...], low)
        partial_out = mm(inflow, oh[:, col]) * carried + diag[:, col]
        yp[:, col] = partial_out
        y = partial_out + mm(coefficient, oh[:, col]) * x[:, col].astype(F32)
        zf = z[:, col].astype(F32)
        gated = y * (zf / (1.0 + jnp.exp(-zf)))
        square = square + gated * gated
        cross = cross + g[:, col].astype(F32) * gain[:, col] * gated
        after = ends[0, :, col] + prefix[0, :, col] * sin[:, col]
        full[0, :, col] = after
        state[:, col] = after
    lane = iota((BLOCK, LANES), 1)
    sums = jnp.where(lane == 0, jnp.sum(square, axis=1, keepdims=True), 0.0)
    stats[...] = sums + jnp.where(lane == 1, jnp.sum(cross, axis=1, keepdims=True), 0.0)


def norm_kernel(lengths, offset, mine, other, cum, step, x, z, g, b, c, yp, dskip, gain, oh, decs, normed, zgrad, dyh, dyl, rho1, rho3, gpart, starts, own_grad, state, *, total_width):
    turn = pl.program_id(0)
    block = pl.num_programs(0) - 1 - turn

    @pl.when(turn == 0)
    def _():
        state[...] = jnp.zeros_like(state)
        gpart[...] = jnp.zeros_like(gpart)

    segment, _, prior, _ = segments(lengths, offset, block)
    inflow = pieces(jnp.exp(cum[...]) * (segment == prior).astype(F32))
    own = jnp.sum(b[...].astype(F32) * c[...].astype(F32), axis=1, keepdims=True)
    coefficient = pieces(head_rows(dskip[...], dskip.shape[1]) + step[...] * own)
    both = mine[...] + other[...]
    mean = both[:, 0:1] / total_width + EPSILON
    scale = lax.rsqrt(mean)
    scale = scale * (1.5 - 0.5 * mean * scale * scale)
    factor = scale * scale * scale * (both[:, 1:2] / total_width)
    first = jnp.zeros((BLOCK, LANES), F32)
    third = jnp.zeros((BLOCK, LANES), F32)
    for at in range(0, x.shape[1], COLS):
        col = slice(at, at + COLS)
        xf = x[:, col].astype(F32)
        partial_out = yp[:, col]
        y = partial_out + mm(coefficient, oh[:, col]) * xf
        zf = z[:, col].astype(F32)
        sigma = 1.0 / (1.0 + jnp.exp(-zf))
        gate = zf * sigma
        gated = y * gate
        scaled = gated * scale
        gf = g[:, col].astype(F32)
        normed[:, col] = (scaled * gain[:, col]).astype(BF16)
        gpart[:, col] += jnp.sum(gf * scaled, axis=0, keepdims=True)
        grad = gf * gain[:, col] * scale - gated * factor
        zgrad[:, col] = (grad * y * (sigma + gate * (1.0 - sigma))).astype(BF16)
        dy = grad * gate
        high, low = split(dy)
        dyh[:, col] = high
        dyl[:, col] = low
        high, low = split(dy * partial_out)
        first = first + (mm_nt(high, oh[:, col]) + mm_nt(low, oh[:, col]))
        high, low = split(dy * xf)
        third = third + (mm_nt(high, oh[:, col]) + mm_nt(low, oh[:, col]))
        high, low = split(dy * mm(inflow, oh[:, col]))
        back = decs[0, :, col] * state[:, col] + (mm_tn(c[...], high) + mm_tn(c[...], low))
        state[:, col] = back
        starts[0, :, col] = back
    rho1[...] = first
    rho3[...] = third

    @pl.when(turn == pl.num_programs(0) - 1)
    def _():
        chunk = own_grad.shape[2]
        for k in range(own_grad.shape[0]):
            own_grad[k] = state[:, k * chunk : (k + 1) * chunk]


def diagonal_back_kernel(lengths, offset, cum, rows, step, x, b, c, dyh, dyl, rho3, sin, full, oh, du, db, dc):
    block = pl.program_id(0)
    seg_column, seg_row, prior, _ = segments(lengths, offset, block)
    mask = (seg_column == seg_row) & (iota((BLOCK, BLOCK), 1) > iota((BLOCK, BLOCK), 0))
    scores = mm_nt(b[...], c[...])
    left = iota((BLOCK, LANES), 1) < HEADDIM
    score_grad = jnp.zeros((BLOCK, BLOCK), F32)
    carried_c = jnp.zeros((BLOCK, STATE), F32)
    inflow = pieces(jnp.exp(cum[...]) * (seg_column == prior).astype(F32))
    for pair in range(x.shape[1] // LANES):
        col = slice(pair * LANES, (pair + 1) * LANES)
        pair_x, high_dy, low_dy = x[:, col], dyh[:, col], dyl[:, col]
        zero = jnp.zeros_like(pair_x)
        x0, x1 = jnp.where(left, pair_x, zero), jnp.where(left, zero, pair_x)
        lhs = jnp.concatenate([jnp.concatenate([x0, x0], axis=1), jnp.concatenate([x1, x1], axis=1)], axis=0)
        products = mm_nt(lhs, jnp.concatenate([high_dy, low_dy], axis=1))
        parts = []
        for e in (0, 1):
            h = 2 * pair + e
            gap = rows[0, h : h + 1, :] - cum[:, h : h + 1]
            decay = jnp.where(mask, jnp.exp(jnp.minimum(gap, 0.0)), 0.0)
            score_grad = score_grad + decay * products[e * BLOCK : (e + 1) * BLOCK] * step[:, h : h + 1]
            parts.append(split(decay * scores))
        high = jnp.concatenate([parts[0][0], parts[1][0]], axis=1)
        low = jnp.concatenate([parts[0][1], parts[1][1]], axis=1)
        both_high = jnp.concatenate([jnp.where(left, high_dy, zero), jnp.where(left, zero, high_dy)], axis=0)
        both_low = jnp.concatenate([jnp.where(left, low_dy, zero), jnp.where(left, zero, low_dy)], axis=0)
        du[:, col] = mm(high, both_high) + (mm(low, both_high) + mm(high, both_low))
    for at in range(0, x.shape[1], COLS):
        col = slice(at, at + COLS)
        dy = dyh[:, col].astype(F32) + dyl[:, col].astype(F32)
        high, low = split(dy * mm(inflow, oh[:, col]))
        entering = jnp.where(block == 0, sin[:, col], full[0, :, col])
        s_high, s_low = split(entering)
        carried_c = carried_c + (mm_nt(high, s_high) + (mm_nt(low, s_high) + mm_nt(high, s_low)))
    lane = iota((BLOCK, LANES), 1)
    own = jnp.sum(jnp.where(lane < GROUP, rho3[...] * step[...], 0.0), axis=1, keepdims=True)
    high, low = split(score_grad)
    db[...] = mm(high, c[...]) + mm(low, c[...]) + own * c[...].astype(F32)
    dc[...] = carried_c + (mm_tn(high, b[...]) + mm_tn(low, b[...])) + own * b[...].astype(F32)


def input_kernel(lengths, offset, sout, starts, decs, full, cum, step, sig, x, b, c, dyh, dyl, diag, rho1, rho3, dskip, alog, oh, dbd, xgrad, db, draw, sums, state, run):
    turn = pl.program_id(0)
    block = pl.num_programs(0) - 1 - turn

    @pl.when(turn == 0)
    def _():
        state[...] = sout[...]
        run[...] = jnp.ones_like(run)
        sums[...] = jnp.zeros_like(sums)

    segment, _, _, last = segments(lengths, offset, block)
    steps = step[...]
    closing = cum[BLOCK - 1 : BLOCK, :]
    tail = pieces(jnp.exp(closing - cum[...]) * (segment == last).astype(F32))
    own = jnp.sum(b[...].astype(F32) * c[...].astype(F32), axis=1, keepdims=True)
    coefficient = pieces(head_rows(dskip[...], dskip.shape[1]) + steps * own)
    step_pieces = pieces(steps)
    second = jnp.zeros((BLOCK, LANES), F32)
    carried_b = jnp.zeros((BLOCK, STATE), F32)
    inner = jnp.zeros((8, LANES), F32)
    for at in range(0, x.shape[1], COLS):
        col = slice(at, at + COLS)
        leaving = state[:, col]
        s_high, s_low = split(leaving)
        weight = mm(tail, oh[:, col])
        step_wide = mm(step_pieces, oh[:, col])
        xf = x[:, col].astype(F32)
        du = diag[:, col] + weight * (mm(b[...], s_high) + mm(b[...], s_low))
        dy = dyh[:, col].astype(F32) + dyl[:, col].astype(F32)
        xgrad[:, col] = (step_wide * du + mm(coefficient, oh[:, col]) * dy).astype(BF16)
        high, low = split(xf * du)
        second = second + (mm_nt(high, oh[:, col]) + mm_nt(low, oh[:, col]))
        high, low = split(xf * (weight * step_wide))
        carried_b = carried_b + (mm_nt(high, s_high) + (mm_nt(low, s_high) + mm_nt(high, s_low)))
        overlap = jnp.sum((full[0, :, col] * leaving).reshape(STATE // 8, 8, COLS), axis=0)
        high, low = split(overlap)
        inner = inner + (mm_nt(high, oh[:, col]) + mm_nt(low, oh[:, col]))
        product = run[:, col] * decs[0, :, col]
        run[:, col] = product
        state[:, col] = starts[0, :, col] + product * sout[:, col]
    db[...] = dbd[...] + carried_b
    upper = (iota((BLOCK, BLOCK), 1) >= iota((BLOCK, BLOCK), 0)).astype(F32)
    rate_grad = jnp.dot(upper, rho1[...] - steps * second, precision=HIGHEST, preferred_element_type=F32)
    rate_grad = rate_grad + jnp.sum(inner, axis=0, keepdims=True)
    speed = jnp.exp(head_rows(alog[...], alog.shape[1]))
    raw_grad = (second + own * rho3[...] - speed * rate_grad) * sig[...]
    draw[...] = raw_grad[:, : draw.shape[1]]
    row = iota((8, LANES), 0)
    bias_row = jnp.where(row == 0, jnp.sum(raw_grad, axis=0, keepdims=True), 0.0)
    alog_row = jnp.where(row == 1, jnp.sum(rate_grad * steps * -speed, axis=0, keepdims=True), 0.0)
    skip_row = jnp.where(row == 2, jnp.sum(rho3[...], axis=0, keepdims=True), 0.0)
    sums[...] += bias_row + alog_row + skip_row


def relay(own, total, axis, forward):
    count = lax.axis_size(axis)
    index = lax.axis_index(axis)
    rank = index if forward else count - 1 - index
    pairs = [(i, i + 1) if forward else (i + 1, i) for i in range(count - 1)]
    chunks = own.shape[0]
    arriving = jnp.zeros(own.shape[1:], F32)
    received = []
    for turn in range(chunks + count - 2):
        at = jnp.clip(turn - rank, 0, chunks - 1)
        message = lax.dynamic_index_in_dim(own, at, 0, False) + lax.dynamic_index_in_dim(total, at, 0, False) * arriving
        arriving = lax.ppermute(message, axis, pairs)
        received.append(arriving)
    stacked = jnp.stack(received)
    picked = [
        lax.dynamic_index_in_dim(stacked, jnp.clip(k + rank - 1, 0, len(received) - 1), 0, False)
        for k in range(chunks)
    ]
    return jnp.concatenate(picked, axis=1)


def shards(x, z, b, c, raw, lengths, bias, alog, dskip, gain, grad):
    _, tokens, width = x.shape
    heads = width // HEADDIM
    blocks = tokens // BLOCK
    chunk = width // CHUNKS
    x, z, grad = (v.reshape(tokens, width) for v in (x, z, grad))
    b, c = b.reshape(tokens, STATE), c.reshape(tokens, STATE)
    raw = raw.reshape(tokens, heads)
    lengths = lengths.reshape(-1)
    bias, alog, dskip = (v.reshape(1, heads) for v in (bias, alog, dskip))
    gain = gain.reshape(1, width)
    offset = jnp.reshape(lax.axis_index("seq") * tokens, (1,)).astype(jnp.int32)
    lane = jnp.arange(LANES)[:, None]
    oh = ((lane % GROUP == jnp.arange(width)[None, :] // HEADDIM) & (lane < 3 * GROUP)).astype(BF16)

    def call(kernel, reverse, ins, outs, scratch, name):
        place = (lambda i: blocks - 1 - i) if reverse else (lambda i: i)

        def spec(kind, shape):
            if kind == "smem":
                return pl.BlockSpec(memory_space=pltpu.SMEM)
            if kind == "tok":
                return pl.BlockSpec((BLOCK, shape[1]), lambda i: (place(i), 0))
            if kind == "blk":
                return pl.BlockSpec((1,) + tuple(shape[1:]), lambda i: (place(i), 0, 0))
            if kind == "prev":
                return pl.BlockSpec((1,) + tuple(shape[1:]), lambda i: (jnp.maximum(place(i) - 1, 0), 0, 0))
            if kind == "row":
                return pl.BlockSpec((2, GROUP, BLOCK), lambda i: (0, 0, place(i)))
            return pl.BlockSpec(tuple(shape), lambda i: (0,) * len(shape))

        return pl.pallas_call(
            kernel,
            grid=(blocks,),
            in_specs=[spec(kind, value.shape) for kind, value in ins],
            out_specs=[spec(kind, shape) for kind, shape, _ in outs],
            out_shape=[jax.ShapeDtypeStruct(shape, dtype) for _, shape, dtype in outs],
            scratch_shapes=[pltpu.VMEM(shape, F32) for shape in scratch],
            compiler_params=pltpu.CompilerParams(
                dimension_semantics=("arbitrary",), vmem_limit_bytes=VMEM_LIMIT
            ),
            name=name,
        )(*[value for _, value in ins])

    wide = (tokens, width)
    narrow = (tokens, LANES)
    states = (blocks, STATE, width)
    line = (blocks, 1, width)
    where = [("smem", lengths), ("smem", offset)]
    e, total, ends, decs, prefix, step, cum, sig, rows = call(
        prepare_kernel, False,
        where + [("tok", raw), ("all", bias), ("all", alog), ("tok", x), ("tok", b), ("all", oh)],
        [("all", (CHUNKS, STATE, chunk), F32), ("all", (CHUNKS, 1, chunk), F32), ("blk", states, F32),
         ("blk", line, F32), ("blk", line, F32), ("tok", narrow, F32), ("tok", narrow, F32), ("tok", narrow, F32),
         ("row", (2, GROUP, tokens), F32)],
        [(STATE, width), (1, width)], "prepare",
    )
    sin = relay(e, total, "seq", True)
    (diag,) = call(
        diagonal_kernel, False,
        where + [("tok", cum), ("row", rows), ("tok", x), ("tok", b), ("tok", c)],
        [("tok", wide, F32)], [], "diagonal",
    )
    yp, stats, full = call(
        output_kernel, False,
        where + [("all", sin), ("blk", ends), ("blk", prefix), ("tok", cum), ("tok", step), ("tok", x), ("tok", z), ("tok", grad),
                 ("tok", b), ("tok", c), ("tok", diag), ("all", dskip), ("all", gain), ("all", oh)],
        [("tok", wide, F32), ("tok", narrow, F32), ("blk", states, F32)],
        [(STATE, width)], "output",
    )
    both = lax.axis_size("head")
    if both == 2:
        other = lax.ppermute(stats, "head", [(0, 1), (1, 0)])
    else:
        other = lax.psum(stats, "head") - stats
    normed, zgrad, dyh, dyl, rho1, rho3, gpart, starts, own_grad = call(
        partial(norm_kernel, total_width=float(width * both)), True,
        where + [("tok", stats), ("tok", other), ("tok", cum), ("tok", step), ("tok", x), ("tok", z), ("tok", grad), ("tok", b),
                 ("tok", c), ("tok", yp), ("all", dskip), ("all", gain), ("all", oh), ("blk", decs)],
        [("tok", wide, BF16), ("tok", wide, BF16), ("tok", wide, BF16), ("tok", wide, BF16), ("tok", narrow, F32),
         ("tok", narrow, F32), ("all", (1, width), F32), ("blk", states, F32), ("all", (CHUNKS, STATE, chunk), F32)],
        [(STATE, width)], "norm",
    )
    sout = relay(own_grad, total, "seq", False)
    du, dbd, dc = call(
        diagonal_back_kernel, False,
        where + [("tok", cum), ("row", rows), ("tok", step), ("tok", x), ("tok", b), ("tok", c), ("tok", dyh), ("tok", dyl),
                 ("tok", rho3), ("all", sin), ("prev", full), ("all", oh)],
        [("tok", wide, F32), ("tok", narrow, F32), ("tok", narrow, F32)], [], "diagonal_back",
    )
    xgrad, db, draw, sums = call(
        input_kernel, True,
        where + [("all", sout), ("blk", starts), ("blk", decs), ("blk", full), ("tok", cum), ("tok", step), ("tok", sig), ("tok", x),
                 ("tok", b), ("tok", c), ("tok", dyh), ("tok", dyl), ("tok", du), ("tok", rho1), ("tok", rho3), ("all", dskip),
                 ("all", alog), ("all", oh), ("tok", dbd)],
        [("tok", wide, BF16), ("tok", narrow, F32), ("tok", (tokens, heads), F32), ("all", (8, LANES), F32)],
        [(STATE, width), (1, width)], "input",
    )
    db, dc = lax.psum((db, dc), "head")
    sums, gpart = lax.psum((sums, gpart), ("seq", "batch"))
    return (
        normed[None],
        xgrad[None],
        zgrad[None],
        db[None],
        dc[None],
        draw[None],
        sums[0, :heads],
        sums[1, :heads],
        sums[2, :heads],
        gpart[0],
    )


def solution(mesh):
    wide = P(("groups", "batch"), "seq", "head")
    shared = P(("groups", "batch"), "seq", None)
    part = P(("groups", "head"))
    head = P("head")
    return jax.shard_map(
        shards,
        mesh=mesh,
        in_specs=(wide, wide, shared, shared, wide, P(("groups", "batch"), None), head, head, head, head, wide),
        out_specs=(wide, wide, wide, shared, shared, wide, part, part, part, part),
        check_vma=False,
    )
```

```python
from functools import partial

import jax
import jax.numpy as jnp
from jax import lax
from jax.experimental import pallas as pl
from jax.experimental.pallas import tpu as pltpu
from jax.sharding import PartitionSpec as P

STATE = 128
HEADDIM = 64
BLOCK = 128
LANES = 128
GROUP = 32
COLS = 256
CHUNKS = 4
LAG = 2
PARTS = 3
EPSILON = 1e-05
HIGHEST = lax.Precision.HIGHEST
F32 = jnp.float32
BF16 = jnp.bfloat16
VMEM_LIMIT = 60 * 1024 * 1024


def mm(a, b):
    return jnp.dot(a, b, preferred_element_type=F32)


def mm_nt(a, b):
    return lax.dot_general(a, b, (((1,), (1,)), ((), ())), preferred_element_type=F32)


def mm_tn(a, b):
    return lax.dot_general(a, b, (((0,), (0,)), ((), ())), preferred_element_type=F32)


def split(value):
    high = value.astype(BF16)
    return high, (value - high.astype(F32)).astype(BF16)


def iota(shape, axis):
    return lax.broadcasted_iota(jnp.int32, shape, axis)


def pieces(value):
    high = value.astype(BF16).astype(F32)
    rest = value - high
    middle = rest.astype(BF16).astype(F32)
    lane = iota(value.shape, 1)
    chosen = jnp.where(lane < GROUP, high, jnp.where(lane < 2 * GROUP, middle, rest - middle))
    return jnp.where(lane < 3 * GROUP, chosen, 0.0).astype(BF16)


def head_rows(spread, heads):
    tile = (iota((heads, LANES), 1) % GROUP == iota((heads, LANES), 0)).astype(F32)
    return jnp.dot(jnp.broadcast_to(spread, (8, heads)), tile, precision=HIGHEST, preferred_element_type=F32)[0:1]


def count_starts(lengths, position):
    start = jnp.int32(0)
    total = (start <= position).astype(jnp.int32)
    for k in range(1, lengths.shape[0]):
        start = start + lengths[k - 1]
        total = total + (start <= position).astype(jnp.int32)
    return total


def segments(lengths, offset, block):
    base = offset[0] + block * BLOCK
    column = count_starts(lengths, base + iota((BLOCK, 1), 0))
    row = count_starts(lengths, base + iota((1, BLOCK), 1))
    return column, row, count_starts(lengths, base - 1), count_starts(lengths, base + BLOCK - 1)


def prepare_kernel(lengths, offset, raw, bias, alog, x, b, oh, e, total, ends, decs, prefix, step, cum, sig, rows, state, run):
    block = pl.program_id(0)
    heads = raw.shape[0]

    @pl.when(block == 0)
    def _():
        state[...] = jnp.zeros_like(state)
        run[...] = jnp.ones_like(run)

    segment, _, prior, last = segments(lengths, offset, block)
    value = raw[...] + bias[...]
    small = jnp.exp(-jnp.abs(value))
    ratio = small / (2.0 + small)
    square = ratio * ratio
    series = jnp.full_like(square, 1.0 / 19.0)
    for odd in (17, 15, 13, 11, 9, 7, 5, 3, 1):
        series = series * square + 1.0 / odd
    soft = jnp.maximum(value, 0.0) + 2.0 * ratio * series
    inverse = 1.0 / (1.0 + small)
    sigma = jnp.where(value >= 0.0, inverse, small * inverse)
    tile = (iota((heads, LANES), 1) % GROUP == iota((heads, LANES), 0)).astype(F32)
    spread = partial(lax.dot_general, dimension_numbers=(((0,), (0,)), ((), ())), precision=HIGHEST, preferred_element_type=F32)
    steps = spread(soft, tile)
    rate = steps * -jnp.exp(head_rows(alog[...], heads))
    lower = (iota((BLOCK, BLOCK), 0) >= iota((BLOCK, BLOCK), 1)).astype(F32)
    cumul = jnp.dot(lower, rate, precision=HIGHEST, preferred_element_type=F32)
    step[...] = steps
    cum[...] = cumul
    sig[...] = spread(sigma, tile)
    rows[0] = cumul.T[:GROUP]
    rows[1, :heads] = soft
    closing = cumul[BLOCK - 1 : BLOCK, :]
    weight = jnp.exp(closing - cumul) * (segment == last).astype(F32) * steps
    decay = jnp.exp(closing) * (last == prior).astype(F32)
    weights = pieces(weight)
    decays = pieces(jnp.broadcast_to(decay, (8, LANES)))
    width = x.shape[1]
    chunk = e.shape[2]
    for at in range(0, width, COLS):
        col = slice(at, at + COLS)
        high, low = split(x[:, col].astype(F32) * mm(weights, oh[:, col]))
        dec = mm(decays, oh[:, col])[0:1]
        fresh = dec * state[:, col] + (mm_tn(b[...], high) + mm_tn(b[...], low))
        state[:, col] = fresh
        ends[0, :, col] = fresh
        decs[0, :, col] = dec
        product = run[:, col] * dec
        run[:, col] = product
        prefix[0, :, col] = product

    @pl.when(block == pl.num_programs(0) - 1)
    def _():
        for c in range(e.shape[0]):
            e[c] = state[:, c * chunk : (c + 1) * chunk]
            total[c] = run[:, c * chunk : (c + 1) * chunk]


def diagonal_kernel(lengths, offset, cum, rows, x, b, c, out):
    block = pl.program_id(0)
    seg_column, seg_row, _, _ = segments(lengths, offset, block)
    mask = (seg_column == seg_row) & (iota((BLOCK, BLOCK), 0) > iota((BLOCK, BLOCK), 1))
    scores = jnp.where(mask, mm_nt(c[...], b[...]), 0.0)
    left = iota((BLOCK, LANES), 1) < HEADDIM
    for pair in range(x.shape[1] // LANES):
        col = slice(pair * LANES, (pair + 1) * LANES)
        parts = []
        for h in (2 * pair, 2 * pair + 1):
            gap = cum[:, h : h + 1] - rows[0, h : h + 1, :]
            parts.append(split(jnp.exp(jnp.minimum(gap, 0.0)) * scores * rows[1, h : h + 1, :]))
        pair_x = x[:, col]
        zero = jnp.zeros_like(pair_x)
        both = jnp.concatenate([jnp.where(left, pair_x, zero), jnp.where(left, zero, pair_x)], axis=0)
        high = jnp.concatenate([parts[0][0], parts[1][0]], axis=1)
        low = jnp.concatenate([parts[0][1], parts[1][1]], axis=1)
        out[:, col] = mm(high, both) + mm(low, both)


def output_kernel(lengths, offset, sin, ends, prefix, cum, step, x, z, g, b, c, diag, dskip, gain, oh, yp, stats, state):
    block = pl.program_id(0)

    @pl.when(block == 0)
    def _():
        state[...] = sin[...]

    segment, _, prior, _ = segments(lengths, offset, block)
    inflow = pieces(jnp.exp(cum[...]) * (segment == prior).astype(F32))
    own = jnp.sum(b[...].astype(F32) * c[...].astype(F32), axis=1, keepdims=True)
    coefficient = pieces(head_rows(dskip[...], dskip.shape[1]) + step[...] * own)
    square = jnp.zeros((BLOCK, COLS), F32)
    cross = jnp.zeros((BLOCK, COLS), F32)
    for at in range(0, x.shape[1], COLS):
        col = slice(at, at + COLS)
        high, low = split(state[:, col])
        carried = mm(c[...], high) + mm(c[...], low)
        partial_out = mm(inflow, oh[:, col]) * carried + diag[:, col]
        yp[:, col] = partial_out
        y = partial_out + mm(coefficient, oh[:, col]) * x[:, col].astype(F32)
        zf = z[:, col].astype(F32)
        gated = y * (zf / (1.0 + jnp.exp(-zf)))
        square = square + gated * gated
        cross = cross + g[:, col].astype(F32) * gain[:, col] * gated
        state[:, col] = ends[0, :, col] + prefix[0, :, col] * sin[:, col]
    lane = iota((BLOCK, LANES), 1)
    sums = jnp.where(lane == 0, jnp.sum(square, axis=1, keepdims=True), 0.0)
    stats[...] = sums + jnp.where(lane == 1, jnp.sum(cross, axis=1, keepdims=True), 0.0)


def norm_kernel(lengths, offset, mine, other, cum, step, x, z, g, b, c, yp, dskip, gain, oh, decs, normed, zgrad, dyh, dyl, rho1, rho3, gpart, starts, own_grad, state, *, total_width):
    turn = pl.program_id(0)
    block = pl.num_programs(0) - 1 - turn

    @pl.when(turn == 0)
    def _():
        state[...] = jnp.zeros_like(state)
        gpart[...] = jnp.zeros_like(gpart)

    segment, _, prior, _ = segments(lengths, offset, block)
    inflow = pieces(jnp.exp(cum[...]) * (segment == prior).astype(F32))
    own = jnp.sum(b[...].astype(F32) * c[...].astype(F32), axis=1, keepdims=True)
    coefficient = pieces(head_rows(dskip[...], dskip.shape[1]) + step[...] * own)
    both = mine[...] + other[...]
    mean = both[:, 0:1] / total_width + EPSILON
    scale = lax.rsqrt(mean)
    scale = scale * (1.5 - 0.5 * mean * scale * scale)
    factor = scale * scale * scale * (both[:, 1:2] / total_width)
    first = jnp.zeros((BLOCK, LANES), F32)
    third = jnp.zeros((BLOCK, LANES), F32)
    for at in range(0, x.shape[1], COLS):
        col = slice(at, at + COLS)
        xf = x[:, col].astype(F32)
        partial_out = yp[:, col]
        y = partial_out + mm(coefficient, oh[:, col]) * xf
        zf = z[:, col].astype(F32)
        sigma = 1.0 / (1.0 + jnp.exp(-zf))
        gate = zf * sigma
        gated = y * gate
        scaled = gated * scale
        gf = g[:, col].astype(F32)
        normed[:, col] = (scaled * gain[:, col]).astype(BF16)
        gpart[:, col] += jnp.sum(gf * scaled, axis=0, keepdims=True)
        grad = gf * gain[:, col] * scale - gated * factor
        zgrad[:, col] = (grad * y * (sigma + gate * (1.0 - sigma))).astype(BF16)
        dy = grad * gate
        high, low = split(dy)
        dyh[:, col] = high
        dyl[:, col] = low
        high, low = split(dy * partial_out)
        first = first + (mm_nt(high, oh[:, col]) + mm_nt(low, oh[:, col]))
        high, low = split(dy * xf)
        third = third + (mm_nt(high, oh[:, col]) + mm_nt(low, oh[:, col]))
        high, low = split(dy * mm(inflow, oh[:, col]))
        back = decs[0, :, col] * state[:, col] + (mm_tn(c[...], high) + mm_tn(c[...], low))
        state[:, col] = back
        starts[0, :, col] = back
    rho1[...] = first
    rho3[...] = third

    @pl.when(turn == pl.num_programs(0) - 1)
    def _():
        chunk = own_grad.shape[2]
        for k in range(own_grad.shape[0]):
            own_grad[k] = state[:, k * chunk : (k + 1) * chunk]


def diagonal_back_kernel(lengths, offset, cum, rows, step, x, b, c, dyh, dyl, sin, ends, prefix, oh, *rest, part, last):
    if last:
        score_in, carried_in, rho3, du, db, dc = rest
    elif part:
        score_in, carried_in, du, score_out, carried_out = rest
    else:
        du, score_out, carried_out = rest
    block = pl.program_id(0)
    seg_column, seg_row, prior, _ = segments(lengths, offset, block)
    mask = (seg_column == seg_row) & (iota((BLOCK, BLOCK), 1) > iota((BLOCK, BLOCK), 0))
    scores = mm_nt(b[...], c[...])
    left = iota((BLOCK, LANES), 1) < HEADDIM
    score_grad = score_in[...] if part else jnp.zeros((BLOCK, BLOCK), F32)
    carried_c = carried_in[...] if part else jnp.zeros((BLOCK, STATE), F32)
    inflow = pieces(jnp.exp(cum[...]) * (seg_column == prior).astype(F32))
    pairs = x.shape[1] // LANES
    for pair in range(pairs):
        col = slice(pair * LANES, (pair + 1) * LANES)
        pair_x, high_dy, low_dy = x[:, col], dyh[:, col], dyl[:, col]
        zero = jnp.zeros_like(pair_x)
        top = jnp.concatenate([jnp.where(left, high_dy, zero), jnp.where(left, low_dy, zero)], axis=1)
        bottom = jnp.concatenate([jnp.where(left, zero, high_dy), jnp.where(left, zero, low_dy)], axis=1)
        both = jnp.concatenate([top, bottom], axis=0)
        products = mm_nt(jnp.concatenate([pair_x, pair_x], axis=1), both)
        parts = []
        for e in (0, 1):
            h = 2 * (part * pairs + pair) + e
            gap = rows[0, h : h + 1, :] - cum[:, h : h + 1]
            decay = jnp.where(mask, jnp.exp(jnp.minimum(gap, 0.0)), 0.0)
            score_grad = score_grad + decay * products[:, e * BLOCK : (e + 1) * BLOCK] * step[:, h : h + 1]
            parts.append(split(decay * scores))
        high = mm(jnp.concatenate([parts[0][0], parts[1][0]], axis=1), both)
        low = mm(jnp.concatenate([parts[0][1], parts[1][1]], axis=1), both[:, :LANES])
        du[:, col] = high[:, :LANES] + (high[:, LANES:] + low)
    for at in range(0, x.shape[1], COLS):
        col = slice(at, at + COLS)
        dy = dyh[:, col].astype(F32) + dyl[:, col].astype(F32)
        high, low = split(dy * mm(inflow, oh[:, col]))
        entering = jnp.where(block == 0, sin[:, col], ends[0, :, col] + prefix[0, :, col] * sin[:, col])
        s_high, s_low = split(entering)
        carried_c = carried_c + (mm_nt(high, s_high) + (mm_nt(low, s_high) + mm_nt(high, s_low)))
    if last:
        lane = iota((BLOCK, LANES), 1)
        own = jnp.sum(jnp.where(lane < GROUP, rho3[...] * step[...], 0.0), axis=1, keepdims=True)
        high, low = split(score_grad)
        db[...] = mm(high, c[...]) + mm(low, c[...]) + own * c[...].astype(F32)
        dc[...] = carried_c + (mm_tn(high, b[...]) + mm_tn(low, b[...])) + own * b[...].astype(F32)
    else:
        score_out[...] = score_grad
        carried_out[...] = carried_c


def input_kernel(lengths, offset, sout, sin, starts, decs, ends, prefix, cum, step, sig, x, b, c, dyh, dyl, diag0, diag1, diag2, rho1, rho3, dskip, alog, oh, dbd, dc_mine, dc_other, gpart, xgrad, db, dc, draw, sums, state, run, small):
    turn = pl.program_id(0)
    block = pl.num_programs(0) - 1 - turn

    @pl.when(turn == 0)
    def _():
        state[...] = sout[...]
        run[...] = jnp.ones_like(run)
        small[...] = jnp.zeros_like(small)

    segment, _, _, last = segments(lengths, offset, block)
    steps = step[...]
    closing = cum[BLOCK - 1 : BLOCK, :]
    tail = pieces(jnp.exp(closing - cum[...]) * (segment == last).astype(F32))
    own = jnp.sum(b[...].astype(F32) * c[...].astype(F32), axis=1, keepdims=True)
    coefficient = pieces(head_rows(dskip[...], dskip.shape[1]) + steps * own)
    step_pieces = pieces(steps)
    second = jnp.zeros((BLOCK, LANES), F32)
    carried_b = jnp.zeros((BLOCK, STATE), F32)
    inner = jnp.zeros((8, LANES), F32)
    for at in range(0, x.shape[1], COLS):
        col = slice(at, at + COLS)
        leaving = state[:, col]
        s_high, s_low = split(leaving)
        weight = mm(tail, oh[:, col])
        step_wide = mm(step_pieces, oh[:, col])
        xf = x[:, col].astype(F32)
        span = x.shape[1] // PARTS
        within = slice(at % span, at % span + COLS)
        du = (diag0, diag1, diag2)[at // span][:, within] + weight * (mm(b[...], s_high) + mm(b[...], s_low))
        dy = dyh[:, col].astype(F32) + dyl[:, col].astype(F32)
        xgrad[:, col] = (step_wide * du + mm(coefficient, oh[:, col]) * dy).astype(BF16)
        high, low = split(xf * du)
        second = second + (mm_nt(high, oh[:, col]) + mm_nt(low, oh[:, col]))
        high, low = split(xf * (weight * step_wide))
        carried_b = carried_b + (mm_nt(high, s_high) + (mm_nt(low, s_high) + mm_nt(high, s_low)))
        whole = ends[0, :, col] + prefix[0, :, col] * sin[:, col]
        overlap = jnp.sum((whole * leaving).reshape(STATE // 8, 8, COLS), axis=0)
        high, low = split(overlap)
        inner = inner + (mm_nt(high, oh[:, col]) + mm_nt(low, oh[:, col]))
        product = run[:, col] * decs[0, :, col]
        run[:, col] = product
        state[:, col] = starts[0, :, col] + product * sout[:, col]
    db[...] = dbd[...] + carried_b
    dc[...] = dc_mine[...] + dc_other[...]
    upper = (iota((BLOCK, BLOCK), 1) >= iota((BLOCK, BLOCK), 0)).astype(F32)
    rate_grad = jnp.dot(upper, rho1[...] - steps * second, precision=HIGHEST, preferred_element_type=F32)
    rate_grad = rate_grad + jnp.sum(inner, axis=0, keepdims=True)
    speed = jnp.exp(head_rows(alog[...], alog.shape[1]))
    raw_grad = (second + own * rho3[...] - speed * rate_grad) * sig[...]
    draw[...] = raw_grad.T[: draw.shape[0]]
    row = iota((8, LANES), 0)
    bias_row = jnp.where(row == 0, jnp.sum(raw_grad, axis=0, keepdims=True), 0.0)
    alog_row = jnp.where(row == 1, jnp.sum(rate_grad * steps * -speed, axis=0, keepdims=True), 0.0)
    skip_row = jnp.where(row == 2, jnp.sum(rho3[...], axis=0, keepdims=True), 0.0)
    small[...] += bias_row + alog_row + skip_row

    @pl.when(turn == pl.num_programs(0) - 1)
    def _():
        for k in range(sums.shape[0]):
            sums[k, :8] = small[...]
            for r in range(x.shape[1] // LANES):
                sums[k, 8 + r : 9 + r] = gpart[:, r * LANES : (r + 1) * LANES]


def relay(own, total, axis, forward, work=None):
    count = lax.axis_size(axis)
    index = lax.axis_index(axis)
    rank = index if forward else count - 1 - index
    chunks = own.shape[0]
    steps = chunks + LAG * (count - 2)
    received = []
    message = None
    for turn in range(steps):
        at = jnp.clip(turn - LAG * rank, 0, chunks - 1)
        mine = lax.dynamic_index_in_dim(own, at, 0, False)
        if turn >= LAG:
            arrived, _ = lax.optimization_barrier((received[turn - LAG], message))
            mine = mine + lax.dynamic_index_in_dim(total, at, 0, False) * arrived
        message = mine
        ranks = [r for r in range(count - 1) if 0 <= turn - LAG * r < chunks]
        pairs = [(r, r + 1) if forward else (count - 1 - r, count - 2 - r) for r in ranks]
        received.append(lax.ppermute(message, axis, pairs))
        if work and turn % LAG == LAG - 1 and turn // LAG < PARTS:
            work(turn // LAG, message)
    stacked = jnp.stack(received)
    picked = [
        lax.dynamic_index_in_dim(stacked, jnp.clip(k + LAG * (rank - 1), 0, steps - 1), 0, False)
        for k in range(chunks)
    ]
    return jnp.where(rank > 0, jnp.concatenate(picked, axis=1), 0.0)


def shards(x, z, b, c, raw, lengths, bias, alog, dskip, gain, grad):
    _, tokens, width = x.shape
    heads = width // HEADDIM
    blocks = tokens // BLOCK
    chunk = width // CHUNKS
    x, z, grad = (v.reshape(tokens, width) for v in (x, z, grad))
    b, c = b.reshape(tokens, STATE), c.reshape(tokens, STATE)
    raw = raw.reshape(tokens, heads).T
    lengths = lengths.reshape(-1)
    bias = bias.reshape(heads, 1)
    alog, dskip = (v.reshape(1, heads) for v in (alog, dskip))
    gain = gain.reshape(1, width)
    offset = jnp.reshape(lax.axis_index("seq") * tokens, (1,)).astype(jnp.int32)
    lane = jnp.arange(LANES)[:, None]
    oh = ((lane % GROUP == jnp.arange(width)[None, :] // HEADDIM) & (lane < 3 * GROUP)).astype(BF16)

    def call(kernel, reverse, ins, outs, scratch, name, part=0):
        place = (lambda i: blocks - 1 - i) if reverse else (lambda i: i)

        def spec(kind, shape):
            if kind == "smem":
                return pl.BlockSpec(memory_space=pltpu.SMEM)
            if kind == "tok":
                return pl.BlockSpec((BLOCK, shape[1]), lambda i: (place(i), 0))
            if kind == "blk":
                return pl.BlockSpec((1,) + tuple(shape[1:]), lambda i: (place(i), 0, 0))
            if kind == "prev":
                return pl.BlockSpec((1,) + tuple(shape[1:]), lambda i: (jnp.maximum(place(i) - 1, 0), 0, 0))
            if kind in ("cols", "hold", "prevs"):
                span = shape[-1] // PARTS
                return {
                    "cols": pl.BlockSpec((BLOCK, span), lambda i: (place(i), part)),
                    "hold": pl.BlockSpec((shape[0], span), lambda i: (0, part)),
                    "prevs": pl.BlockSpec((1, shape[1], span), lambda i: (jnp.maximum(place(i) - 1, 0), 0, part)),
                }[kind]
            if kind == "raw":
                return pl.BlockSpec((shape[0], BLOCK), lambda i: (0, place(i)))
            if kind == "row":
                return pl.BlockSpec((2, GROUP, BLOCK), lambda i: (0, 0, place(i)))
            return pl.BlockSpec(tuple(shape), lambda i: (0,) * len(shape))

        return pl.pallas_call(
            kernel,
            grid=(blocks,),
            in_specs=[spec(kind, value.shape) for kind, value in ins],
            out_specs=[spec(kind, shape) for kind, shape, _ in outs],
            out_shape=[jax.ShapeDtypeStruct(shape, dtype) for _, shape, dtype in outs],
            scratch_shapes=[pltpu.VMEM(shape, F32) for shape in scratch],
            compiler_params=pltpu.CompilerParams(
                dimension_semantics=("arbitrary",), vmem_limit_bytes=VMEM_LIMIT
            ),
            name=name,
        )(*[value for _, value in ins])

    wide = (tokens, width)
    narrow = (tokens, LANES)
    states = (blocks, STATE, width)
    line = (blocks, 1, width)
    where = [("smem", lengths), ("smem", offset)]
    e, total, ends, decs, prefix, step, cum, sig, rows = call(
        prepare_kernel, False,
        where + [("raw", raw), ("all", bias), ("all", alog), ("tok", x), ("tok", b), ("all", oh)],
        [("all", (CHUNKS, STATE, chunk), F32), ("all", (CHUNKS, 1, chunk), F32), ("blk", states, F32),
         ("blk", line, F32), ("blk", line, F32), ("tok", narrow, F32), ("tok", narrow, F32), ("tok", narrow, F32),
         ("row", (2, GROUP, tokens), F32)],
        [(STATE, width), (1, width)], "prepare",
    )
    sin = relay(e, total, "seq", True)
    (diag,) = call(
        diagonal_kernel, False,
        where + [("tok", cum), ("row", rows), ("tok", x), ("tok", b), ("tok", c)],
        [("tok", wide, F32)], [], "diagonal",
    )
    yp, stats = call(
        output_kernel, False,
        where + [("all", sin), ("blk", ends), ("blk", prefix), ("tok", cum), ("tok", step), ("tok", x), ("tok", z), ("tok", grad),
                 ("tok", b), ("tok", c), ("tok", diag), ("all", dskip), ("all", gain), ("all", oh)],
        [("tok", wide, F32), ("tok", narrow, F32)],
        [(STATE, width)], "output",
    )
    both = lax.axis_size("head")
    exchange = partial(lax.ppermute, axis_name="head", perm=[(0, 1), (1, 0)])
    other = exchange(stats)
    normed, zgrad, dyh, dyl, rho1, rho3, gpart, starts, own_grad = call(
        partial(norm_kernel, total_width=float(width * both)), True,
        where + [("tok", stats), ("tok", other), ("tok", cum), ("tok", step), ("tok", x), ("tok", z), ("tok", grad), ("tok", b),
                 ("tok", c), ("tok", yp), ("all", dskip), ("all", gain), ("all", oh), ("blk", decs)],
        [("tok", wide, BF16), ("tok", wide, BF16), ("tok", wide, BF16), ("tok", wide, BF16), ("tok", narrow, F32),
         ("tok", narrow, F32), ("all", (1, width), F32), ("blk", states, F32), ("all", (CHUNKS, STATE, chunk), F32)],
        [(STATE, width)], "norm",
    )
    du, carry = [], []

    def back_part(part, message):
        last = part == PARTS - 1
        high, low = dyh, dyl
        if part:
            high, low, _ = lax.optimization_barrier((dyh, dyl, message))
        span = width // PARTS
        out = call(
            partial(diagonal_back_kernel, part=part, last=last), False,
            where + [("tok", cum), ("row", rows), ("tok", step), ("cols", x), ("tok", b), ("tok", c), ("cols", high), ("cols", low),
                     ("hold", sin), ("prevs", ends), ("prevs", prefix), ("hold", oh)]
            + [("tok", value) for value in carry] + ([("tok", rho3)] if last else []),
            [("tok", (tokens, span), F32), ("tok", narrow, F32), ("tok", narrow, F32)], [], "diagonal_back", part,
        )
        du.append(out[0])
        carry[:] = out[1:]

    sout = relay(own_grad, total, "seq", False, back_part)
    dbd, dc = carry
    dc_other = exchange(dc)
    members = lax.axis_size(("seq", "batch"))
    xgrad, db, dc, draw, sums = call(
        input_kernel, True,
        where + [("all", sout), ("all", sin), ("blk", starts), ("blk", decs), ("blk", ends), ("blk", prefix), ("tok", cum), ("tok", step),
                 ("tok", sig), ("tok", x), ("tok", b), ("tok", c), ("tok", dyh), ("tok", dyl), ("tok", du[0]), ("tok", du[1]), ("tok", du[2]), ("tok", rho1), ("tok", rho3),
                 ("all", dskip), ("all", alog), ("all", oh), ("tok", dbd), ("tok", dc), ("tok", dc_other), ("all", gpart)],
        [("tok", wide, BF16), ("tok", narrow, F32), ("tok", narrow, F32), ("raw", (heads, tokens), F32),
         ("all", (members, 8 + width // LANES, LANES), F32)],
        [(STATE, width), (1, width), (8, LANES)], "input",
    )
    db = db + exchange(db)
    sums = jnp.sum(lax.all_to_all(sums, ("seq", "batch"), 0, 0), axis=0)
    return (
        normed[None],
        xgrad[None],
        zgrad[None],
        db[None],
        dc[None],
        draw.T[None],
        sums[0, :heads],
        sums[1, :heads],
        sums[2, :heads],
        sums[8:].reshape(width),
    )


def solution(mesh):
    wide = P(("groups", "batch"), "seq", "head")
    shared = P(("groups", "batch"), "seq", None)
    part = P(("groups", "head"))
    head = P("head")
    return jax.shard_map(
        shards,
        mesh=mesh,
        in_specs=(wide, wide, shared, shared, wide, P(("groups", "batch"), None), head, head, head, head, wide),
        out_specs=(wide, wide, wide, shared, shared, wide, part, part, part, part),
        check_vma=False,
    )
```

```python
from functools import partial

import jax
import jax.numpy as jnp
import numpy as np
from jax import lax
from jax.experimental import pallas as pl
from jax.experimental.pallas import tpu as pltpu
from jax.sharding import PartitionSpec as P

STATE = 128
HEADDIM = 64
BLOCK = 128
LANES = 128
GROUP = 32
COLS = 256
HALF_CHUNKS = 2
LAG = 2
EPSILON = 1e-05
HIGHEST = lax.Precision.HIGHEST
F32 = jnp.float32
BF16 = jnp.bfloat16
VMEM_LIMIT = 60 * 1024 * 1024


def mm(a, b):
    return jnp.dot(a, b, preferred_element_type=F32)


def mm_nt(a, b):
    return lax.dot_general(a, b, (((1,), (1,)), ((), ())), preferred_element_type=F32)


def mm_tn(a, b):
    return lax.dot_general(a, b, (((0,), (0,)), ((), ())), preferred_element_type=F32)


def split(value):
    high = value.astype(BF16)
    return high, (value - high.astype(F32)).astype(BF16)


def iota(shape, axis):
    return lax.broadcasted_iota(jnp.int32, shape, axis)


def pieces(value):
    high = value.astype(BF16).astype(F32)
    rest = value - high
    middle = rest.astype(BF16).astype(F32)
    lane = iota(value.shape, 1)
    chosen = jnp.where(lane < GROUP, high, jnp.where(lane < 2 * GROUP, middle, rest - middle))
    return jnp.where(lane < 3 * GROUP, chosen, 0.0).astype(BF16)


def head_rows(spread, heads):
    tile = (iota((heads, LANES), 1) % GROUP == iota((heads, LANES), 0)).astype(F32)
    return jnp.dot(jnp.broadcast_to(spread, (8, heads)), tile, precision=HIGHEST, preferred_element_type=F32)[0:1]


def count_starts(lengths, position):
    start = jnp.int32(0)
    total = (start <= position).astype(jnp.int32)
    for k in range(1, lengths.shape[0]):
        start = start + lengths[k - 1]
        total = total + (start <= position).astype(jnp.int32)
    return total


def segments(lengths, offset, block):
    base = offset[0] + block * BLOCK
    column = count_starts(lengths, base + iota((BLOCK, 1), 0))
    row = count_starts(lengths, base + iota((1, BLOCK), 1))
    return column, row, count_starts(lengths, base - 1), count_starts(lengths, base + BLOCK - 1)


def local_states(weights, decays, x, b, oh, e, total, ends, decs, prefix, state, run):
    for at in range(0, x.shape[1], COLS):
        col = slice(at, at + COLS)
        high, low = split(x[:, col].astype(F32) * mm(weights, oh[:, col]))
        dec = mm(decays, oh[:, col])[0:1]
        fresh = dec * state[:, col] + (mm_tn(b[...], high) + mm_tn(b[...], low))
        state[:, col] = fresh
        ends[0, :, col] = fresh
        decs[0, :, col] = dec
        product = run[:, col] * dec
        run[:, col] = product
        prefix[0, :, col] = product

    @pl.when(pl.program_id(0) == pl.num_programs(0) - 1)
    def _():
        chunk = e.shape[2]
        for k in range(e.shape[0]):
            e[k] = state[:, k * chunk : (k + 1) * chunk]
            total[k] = run[:, k * chunk : (k + 1) * chunk]


def clear_states(state, run):
    @pl.when(pl.program_id(0) == 0)
    def _():
        state[...] = jnp.zeros_like(state)
        run[...] = jnp.ones_like(run)


def weigh(cumul, steps, segment, prior, last):
    closing = cumul[BLOCK - 1 : BLOCK, :]
    weight = jnp.exp(closing - cumul) * (segment == last).astype(F32) * steps
    decay = jnp.exp(closing) * (last == prior).astype(F32)
    return pieces(weight), pieces(jnp.broadcast_to(decay, (8, LANES)))


def prepare_kernel(lengths, offset, raw, bias, alog, x, b, oh, e, total, ends, decs, prefix, step, cum, sig, rows, state, run):
    heads = raw.shape[0]
    clear_states(state, run)
    segment, _, prior, last = segments(lengths, offset, pl.program_id(0))
    same = iota((heads, heads), 0) == iota((heads, heads), 1)
    shift = jnp.sum(jnp.where(same, jnp.broadcast_to(bias[...], (heads, heads)), 0.0), axis=1, keepdims=True)
    value = raw[...] + shift
    small = jnp.exp(-jnp.abs(value))
    ratio = small / (2.0 + small)
    square = ratio * ratio
    series = jnp.full_like(square, 1.0 / 19.0)
    for odd in (17, 15, 13, 11, 9, 7, 5, 3, 1):
        series = series * square + 1.0 / odd
    soft = jnp.maximum(value, 0.0) + 2.0 * ratio * series
    inverse = 1.0 / (1.0 + small)
    sigma = jnp.where(value >= 0.0, inverse, small * inverse)
    tile = (iota((heads, LANES), 1) % GROUP == iota((heads, LANES), 0)).astype(F32)
    spread = partial(lax.dot_general, dimension_numbers=(((0,), (0,)), ((), ())), precision=HIGHEST, preferred_element_type=F32)
    steps = spread(soft, tile)
    rate = steps * -jnp.exp(head_rows(alog[...], heads))
    lower = (iota((BLOCK, BLOCK), 0) >= iota((BLOCK, BLOCK), 1)).astype(F32)
    cumul = jnp.dot(lower, rate, precision=HIGHEST, preferred_element_type=F32)
    step[...] = steps
    cum[...] = cumul
    sig[...] = spread(sigma, tile)
    rows[0] = cumul.T[:GROUP]
    rows[1] = steps.T[:GROUP]
    weights, decays = weigh(cumul, steps, segment, prior, last)
    local_states(weights, decays, x, b, oh, e, total, ends, decs, prefix, state, run)


def states_kernel(lengths, offset, cum, step, x, b, oh, e, total, ends, decs, prefix, state, run):
    clear_states(state, run)
    segment, _, prior, last = segments(lengths, offset, pl.program_id(0))
    weights, decays = weigh(cum[...], step[...], segment, prior, last)
    local_states(weights, decays, x, b, oh, e, total, ends, decs, prefix, state, run)


def diagonal_kernel(lengths, offset, cum, rows, x, b, c, out, *, first):
    block = pl.program_id(0)
    seg_column, seg_row, _, _ = segments(lengths, offset, block)
    mask = (seg_column == seg_row) & (iota((BLOCK, BLOCK), 0) > iota((BLOCK, BLOCK), 1))
    scores = jnp.where(mask, mm_nt(c[...], b[...]), 0.0)
    left = iota((BLOCK, LANES), 1) < HEADDIM
    for pair in range(x.shape[1] // LANES):
        col = slice(pair * LANES, (pair + 1) * LANES)
        parts = []
        for h in (first + 2 * pair, first + 2 * pair + 1):
            gap = cum[:, h : h + 1] - rows[0, h : h + 1, :]
            parts.append(split(jnp.exp(jnp.minimum(gap, 0.0)) * scores * rows[1, h : h + 1, :]))
        pair_x = x[:, col]
        zero = jnp.zeros_like(pair_x)
        both = jnp.concatenate([jnp.where(left, pair_x, zero), jnp.where(left, zero, pair_x)], axis=0)
        high = jnp.concatenate([parts[0][0], parts[1][0]], axis=1)
        low = jnp.concatenate([parts[0][1], parts[1][1]], axis=1)
        out[:, col] = mm(high, both) + mm(low, both)


def output_kernel(lengths, offset, sin, ends, prefix, cum, step, x, z, g, b, c, diag, dskip, gain, oh, before, yp, stats, state):
    block = pl.program_id(0)

    @pl.when(block == 0)
    def _():
        state[...] = sin[...]

    segment, _, prior, _ = segments(lengths, offset, block)
    inflow = pieces(jnp.exp(cum[...]) * (segment == prior).astype(F32))
    own = jnp.sum(b[...].astype(F32) * c[...].astype(F32), axis=1, keepdims=True)
    coefficient = pieces(head_rows(dskip[...], dskip.shape[1]) + step[...] * own)
    square = jnp.zeros((BLOCK, COLS), F32)
    cross = jnp.zeros((BLOCK, COLS), F32)
    for at in range(0, x.shape[1], COLS):
        col = slice(at, at + COLS)
        high, low = split(state[:, col])
        carried = mm(c[...], high) + mm(c[...], low)
        partial_out = mm(inflow, oh[:, col]) * carried + diag[:, col]
        yp[:, col] = partial_out
        y = partial_out + mm(coefficient, oh[:, col]) * x[:, col].astype(F32)
        zf = z[:, col].astype(F32)
        gated = y * (zf / (1.0 + jnp.exp(-zf)))
        square = square + gated * gated
        cross = cross + g[:, col].astype(F32) * gain[:, col] * gated
        state[:, col] = ends[0, :, col] + prefix[0, :, col] * sin[:, col]
    lane = iota((BLOCK, LANES), 1)
    sums = jnp.where(lane == 0, jnp.sum(square, axis=1, keepdims=True), 0.0)
    sums = sums + jnp.where(lane == 1, jnp.sum(cross, axis=1, keepdims=True), 0.0)
    stats[...] = sums if before is None else before[...] + sums


def norm_kernel(lengths, offset, mine, other, cum, step, x, z, g, b, c, yp, dskip, gain, oh, decs, _n, _z, normed, zgrad, dyh, dyl, gpart, starts, own_grad, state, *, total_width):
    turn = pl.program_id(0)
    block = pl.num_programs(0) - 1 - turn

    @pl.when(turn == 0)
    def _():
        state[...] = jnp.zeros_like(state)
        gpart[...] = jnp.zeros_like(gpart)

    segment, _, prior, _ = segments(lengths, offset, block)
    inflow = pieces(jnp.exp(cum[...]) * (segment == prior).astype(F32))
    own = jnp.sum(b[...].astype(F32) * c[...].astype(F32), axis=1, keepdims=True)
    coefficient = pieces(head_rows(dskip[...], dskip.shape[1]) + step[...] * own)
    both = mine[...] + other[...]
    mean = both[:, 0:1] / total_width + EPSILON
    scale = lax.rsqrt(mean)
    scale = scale * (1.5 - 0.5 * mean * scale * scale)
    factor = scale * scale * scale * (both[:, 1:2] / total_width)
    for at in range(0, x.shape[1], COLS):
        col = slice(at, at + COLS)
        xf = x[:, col].astype(F32)
        y = yp[:, col] + mm(coefficient, oh[:, col]) * xf
        zf = z[:, col].astype(F32)
        sigma = 1.0 / (1.0 + jnp.exp(-zf))
        gate = zf * sigma
        gated = y * gate
        scaled = gated * scale
        gf = g[:, col].astype(F32)
        normed[:, col] = (scaled * gain[:, col]).astype(BF16)
        gpart[:, col] += jnp.sum(gf * scaled, axis=0, keepdims=True)
        grad = gf * gain[:, col] * scale - gated * factor
        zgrad[:, col] = (grad * y * (sigma + gate * (1.0 - sigma))).astype(BF16)
        dy = grad * gate
        high, low = split(dy)
        dyh[:, col] = high
        dyl[:, col] = low
        high, low = split(dy * mm(inflow, oh[:, col]))
        back = decs[0, :, col] * state[:, col] + (mm_tn(c[...], high) + mm_tn(c[...], low))
        state[:, col] = back
        starts[0, :, col] = back

    @pl.when(turn == pl.num_programs(0) - 1)
    def _():
        chunk = own_grad.shape[2]
        for k in range(own_grad.shape[0]):
            own_grad[k] = state[:, k * chunk : (k + 1) * chunk]


def diagonal_back_kernel(lengths, offset, cum, rows, step, x, b, c, dyh, dyl, yp, sin, ends, prefix, oh, dskip, *rest, part, last):
    count = 5 if part else 0
    before, xpart, after = rest[:count], rest[count], rest[count + 1 :]
    block = pl.program_id(0)
    seg_column, seg_row, prior, _ = segments(lengths, offset, block)
    mask = (seg_column == seg_row) & (iota((BLOCK, BLOCK), 1) > iota((BLOCK, BLOCK), 0))
    scores = mm_nt(b[...], c[...])
    left = iota((BLOCK, LANES), 1) < HEADDIM
    sums = [value[...] for value in before] if part else [jnp.zeros((BLOCK, LANES), F32)] * 5
    score_grad, carried_c, rho1, rho2, rho3 = sums
    own_score = jnp.sum(b[...].astype(F32) * c[...].astype(F32), axis=1, keepdims=True)
    coefficient = pieces(head_rows(dskip[...], dskip.shape[1]) + step[...] * own_score)
    step_pieces = pieces(step[...])
    du_pairs = []
    inflow = pieces(jnp.exp(cum[...]) * (seg_column == prior).astype(F32))
    pairs = x.shape[1] // LANES
    for pair in range(pairs):
        col = slice(pair * LANES, (pair + 1) * LANES)
        pair_x, high_dy, low_dy = x[:, col], dyh[:, col], dyl[:, col]
        zero = jnp.zeros_like(pair_x)
        top = jnp.concatenate([jnp.where(left, high_dy, zero), jnp.where(left, low_dy, zero)], axis=1)
        bottom = jnp.concatenate([jnp.where(left, zero, high_dy), jnp.where(left, zero, low_dy)], axis=1)
        both = jnp.concatenate([top, bottom], axis=0)
        products = mm_nt(jnp.concatenate([pair_x, pair_x], axis=1), both)
        parts = []
        for e in (0, 1):
            h = 2 * (part * pairs + pair) + e
            gap = rows[0, h : h + 1, :] - cum[:, h : h + 1]
            decay = jnp.where(mask, jnp.exp(jnp.minimum(gap, 0.0)), 0.0)
            score_grad = score_grad + decay * products[:, e * BLOCK : (e + 1) * BLOCK] * step[:, h : h + 1]
            parts.append(split(decay * scores))
        high = mm(jnp.concatenate([parts[0][0], parts[1][0]], axis=1), both)
        low = mm(jnp.concatenate([parts[0][1], parts[1][1]], axis=1), both[:, :LANES])
        du_pairs.append(high[:, :LANES] + (high[:, LANES:] + low))
    dy = dyh[...].astype(F32) + dyl[...].astype(F32)
    du = jnp.concatenate(du_pairs, axis=1)
    xf = x[...].astype(F32)
    high, low = split(dy * mm(inflow, oh[...]))
    entering = jnp.where(block == 0, sin[...], ends[0] + prefix[0] * sin[...])
    s_high, s_low = split(entering)
    carried_c = carried_c + (mm_nt(high, s_high) + (mm_nt(low, s_high) + mm_nt(high, s_low)))
    xpart[...] = mm(step_pieces, oh[...]) * du + mm(coefficient, oh[...]) * dy
    high, low = split(dy * yp[...])
    rho1 = rho1 + (mm_nt(high, oh[...]) + mm_nt(low, oh[...]))
    high, low = split(xf * du)
    rho2 = rho2 + (mm_nt(high, oh[...]) + mm_nt(low, oh[...]))
    high, low = split(dy * xf)
    rho3 = rho3 + (mm_nt(high, oh[...]) + mm_nt(low, oh[...]))
    if last:
        lane = iota((BLOCK, LANES), 1)
        own = jnp.sum(jnp.where(lane < GROUP, rho3 * step[...], 0.0), axis=1, keepdims=True)
        high, low = split(score_grad)
        score_grad = mm(high, c[...]) + mm(low, c[...]) + own * c[...].astype(F32)
        carried_c = carried_c + (mm_tn(high, b[...]) + mm_tn(low, b[...])) + own * b[...].astype(F32)
    for ref, value in zip(after, (score_grad, carried_c, rho1, rho2, rho3)):
        ref[...] = value


def input_kernel(lengths, offset, sout, sin, starts, decs, ends, prefix, cum, step, x, b, part0, part1, oh, *rest, final):
    if final:
        _, db_in, scaled_in, inner_in, c, rho1, rho2, rho3, sig, alog, dbd, dc_mine, dc_other, gpart0, gpart1 = rest[:15]
        xgrad, db, dc, draw, sums, state, run, small = rest[15:]
    else:
        xgrad, db, scaled_out, inner_out, state, run = rest
    turn = pl.program_id(0)
    block = pl.num_programs(0) - 1 - turn

    @pl.when(turn == 0)
    def _():
        state[...] = sout[...]
        run[...] = jnp.ones_like(run)
        if final:
            small[...] = jnp.zeros_like(small)

    segment, _, prior, last = segments(lengths, offset, block)
    steps = step[...]
    weights, _ = weigh(cum[...], steps, segment, prior, last)
    scaled = scaled_in[...] if final else jnp.zeros((BLOCK, LANES), F32)
    carried_b = db_in[...] if final else jnp.zeros((BLOCK, STATE), F32)
    inner = inner_in[0] if final else jnp.zeros((8, LANES), F32)
    span = part0.shape[1]
    for at, part in ((0, part0), (span, part1)):
        col = slice(at, at + span)
        leaving = state[:, col]
        s_high, s_low = split(leaving)
        wide = mm(weights, oh[:, col])
        xf = x[:, col].astype(F32)
        du = wide * (mm(b[...], s_high) + mm(b[...], s_low))
        xgrad[:, col] = (part[...] + du).astype(BF16)
        high, low = split(xf * du)
        scaled = scaled + (mm_nt(high, oh[:, col]) + mm_nt(low, oh[:, col]))
        high, low = split(xf * wide)
        carried_b = carried_b + (mm_nt(high, s_high) + (mm_nt(low, s_high) + mm_nt(high, s_low)))
        whole = ends[0, :, col] + prefix[0, :, col] * sin[:, col]
        overlap = jnp.sum((whole * leaving).reshape(STATE // 8, 8, span), axis=0)
        high, low = split(overlap)
        inner = inner + (mm_nt(high, oh[:, col]) + mm_nt(low, oh[:, col]))
        product = run[:, col] * decs[0, :, col]
        run[:, col] = product
        state[:, col] = starts[0, :, col] + product * sout[:, col]
    if not final:
        db[...] = carried_b
        scaled_out[...] = scaled
        inner_out[0] = inner
        return
    db[...] = dbd[...] + carried_b
    dc[...] = dc_mine[...] + dc_other[...]
    own = jnp.sum(b[...].astype(F32) * c[...].astype(F32), axis=1, keepdims=True)
    second = rho2[...] + jnp.where(steps > 0.0, scaled / steps, 0.0)
    upper = (iota((BLOCK, BLOCK), 1) >= iota((BLOCK, BLOCK), 0)).astype(F32)
    rate_grad = jnp.dot(upper, rho1[...] - steps * rho2[...] - scaled, precision=HIGHEST, preferred_element_type=F32)
    rate_grad = rate_grad + jnp.sum(inner, axis=0, keepdims=True)
    speed = jnp.exp(head_rows(alog[...], alog.shape[1]))
    raw_grad = (second + own * rho3[...] - speed * rate_grad) * sig[...]
    draw[...] = raw_grad.T[: draw.shape[0]]
    row = iota((8, LANES), 0)
    bias_row = jnp.where(row == 0, jnp.sum(raw_grad, axis=0, keepdims=True), 0.0)
    alog_row = jnp.where(row == 1, jnp.sum(rate_grad * steps * -speed, axis=0, keepdims=True), 0.0)
    skip_row = jnp.where(row == 2, jnp.sum(rho3[...], axis=0, keepdims=True), 0.0)
    small[...] += bias_row + alog_row + skip_row

    @pl.when(turn == pl.num_programs(0) - 1)
    def _():
        rows = gpart0.shape[1] // LANES
        for k in range(sums.shape[0]):
            sums[k, :8] = small[...]
            for r in range(rows):
                sums[k, 8 + r : 9 + r] = gpart0[:, r * LANES : (r + 1) * LANES]
                sums[k, 8 + rows + r : 9 + rows + r] = gpart1[:, r * LANES : (r + 1) * LANES]


def relay(own, total, axis, forward, work):
    count = lax.axis_size(axis)
    index = lax.axis_index(axis)
    rank = index if forward else count - 1 - index
    chunks = 2 * HALF_CHUNKS
    steps = chunks + LAG * (count - 2)
    received, halves, message = [], None, None

    def chunk(pair, at):
        picked = [lax.dynamic_index_in_dim(v, jnp.clip(at - k * HALF_CHUNKS, 0, HALF_CHUNKS - 1), 0, False) for k, v in enumerate(pair)]
        return jnp.where(at < HALF_CHUNKS, picked[0], picked[1])

    def half(which):
        turns = received[: steps - LAG] if which == 0 else received
        stacked = jnp.stack(turns)
        at = [k + which * HALF_CHUNKS + LAG * (rank - 1) for k in range(HALF_CHUNKS)]
        picked = [lax.dynamic_index_in_dim(stacked, jnp.clip(k, 0, len(turns) - 1), 0, False) for k in at]
        return jnp.where(rank > 0, jnp.concatenate(picked, axis=1), 0.0)

    for turn in range(steps):
        if turn < LAG:
            mine = own[turn]
            if message is not None:
                mine, _ = lax.optimization_barrier((mine, message))
        else:
            at = jnp.clip(turn - LAG * rank, 0, chunks - 1)
            arrived, _ = lax.optimization_barrier((received[turn - LAG], message))
            mine = chunk(halves[0], at) + chunk(halves[1], at) * arrived
        message = mine
        ranks = [r for r in range(count - 1) if 0 <= turn - LAG * r < chunks]
        pairs = [(r, r + 1) if forward else (count - 1 - r, count - 2 - r) for r in ranks]
        received.append(lax.ppermute(message, axis, pairs))
        if turn == LAG - 1:
            second = work(0, message, None)
            halves = (own, second[0]), (total, second[1])
        elif turn == steps - 1:
            first = half(0)
            work(-1, message, first)
        elif turn % LAG == LAG - 1 and turn < 6:
            work(turn // LAG, message, None)
    return first, half(1)


def one_hot(width):
    lane = np.arange(LANES)[:, None]
    return np.logical_and(lane % GROUP == np.arange(width)[None, :] // HEADDIM, lane < 3 * GROUP)


def shards(x, z, b, c, raw, lengths, bias, alog, dskip, gain, grad):
    _, tokens, width = x.shape
    heads = width // HEADDIM
    blocks = tokens // BLOCK
    span, quarter = width // 2, width // 4
    chunk = span // HALF_CHUNKS
    x, z, grad = (v.reshape(tokens, width) for v in (x, z, grad))
    b, c = b.reshape(tokens, STATE), c.reshape(tokens, STATE)
    raw = raw.reshape(tokens, heads).T
    lengths = lengths.reshape(-1)
    bias, alog, dskip = (v.reshape(1, heads) for v in (bias, alog, dskip))
    gain = gain.reshape(1, width)
    offset = jnp.reshape(lax.axis_index("seq") * tokens, (1,)).astype(jnp.int32)
    oh = jnp.asarray(one_hot(width), BF16)

    def tied(message):
        return [("smem", lengths), ("smem", lax.optimization_barrier((offset, message))[0])]

    def call(kernel, reverse, ins, outs, scratch, name, aliases=None):
        place = (lambda i: blocks - 1 - i) if reverse else (lambda i: i)

        def spec(kind, shape):
            kind, step, at = kind if isinstance(kind, tuple) else (kind, shape[-1], 0)
            if kind == "smem":
                return pl.BlockSpec(memory_space=pltpu.SMEM)
            if kind == "any":
                return pl.BlockSpec(memory_space=pl.ANY)
            if kind == "tok":
                return pl.BlockSpec((BLOCK, step), lambda i: (place(i), at))
            if kind == "blk":
                return pl.BlockSpec((1, shape[1], step), lambda i: (place(i), 0, at))
            if kind == "prev":
                return pl.BlockSpec((1, shape[1], step), lambda i: (jnp.maximum(place(i) - 1, 0), 0, at))
            if kind == "raw":
                return pl.BlockSpec((shape[0], BLOCK), lambda i: (0, place(i)))
            if kind == "row":
                return pl.BlockSpec((2, GROUP, BLOCK), lambda i: (0, 0, place(i)))
            return pl.BlockSpec(tuple(shape[:-1]) + (step,), lambda i: (0,) * (len(shape) - 1) + (at,))

        return pl.pallas_call(
            kernel,
            grid=(blocks,),
            in_specs=[spec(kind, value.shape) for kind, value in ins],
            out_specs=[spec(kind, shape) for kind, shape, _ in outs],
            out_shape=[jax.ShapeDtypeStruct(shape, dtype) for _, shape, dtype in outs],
            scratch_shapes=[pltpu.VMEM(shape, F32) for shape in scratch],
            input_output_aliases=aliases or {},
            compiler_params=pltpu.CompilerParams(
                dimension_semantics=("arbitrary",), vmem_limit_bytes=VMEM_LIMIT
            ),
            name=name,
        )(*[value for _, value in ins])

    wide = (tokens, width)
    half = (tokens, span)
    narrow = (tokens, LANES)
    states = (blocks, STATE, span)
    line = (blocks, 1, span)
    own_outs = [("all", (HALF_CHUNKS, STATE, chunk), F32), ("all", (HALF_CHUNKS, 1, chunk), F32), ("blk", states, F32),
                ("blk", line, F32), ("blk", line, F32)]
    first = call(
        prepare_kernel, False,
        [("smem", lengths), ("smem", offset), ("raw", raw), ("all", bias), ("all", alog), (("tok", span, 0), x), ("tok", b), (("all", span, 0), oh)],
        own_outs + [("tok", narrow, F32), ("tok", narrow, F32), ("tok", narrow, F32), ("row", (2, GROUP, tokens), F32)],
        [(STATE, span), (1, span)], "prepare",
    )
    step, cum, sig, rows = first[5:]
    locals_ = [first[:5], None]
    diag, sin, yp, stats = [None, None], [None, None], [None, None], None

    def diagonal(where, h):
        (diag[h],) = call(
            partial(diagonal_kernel, first=h * heads // 2), False,
            where + [("tok", cum), ("row", rows), (("tok", span, h), x), ("tok", b), ("tok", c)],
            [("tok", half, F32)], [], "diagonal",
        )

    def output(where, h):
        kernel = output_kernel if h else (lambda *refs: output_kernel(*refs[:16], None, *refs[16:]))
        _, _, ends, _, prefix = locals_[h]
        yp[h], total = call(
            kernel, False,
            where + [("all", sin[h]), ("blk", ends), ("blk", prefix), ("tok", cum), ("tok", step)]
            + [(("tok", span, h), v) for v in (x, z, grad)]
            + [("tok", b), ("tok", c), ("tok", diag[h]), ("all", dskip), (("all", span, h), gain), (("all", span, h), oh)]
            + ([("tok", stats)] if h else []),
            [("tok", half, F32), ("tok", narrow, F32)], [(STATE, span)], "output",
        )
        return total

    def forward_work(slot, message, arrived):
        nonlocal stats
        where = tied(message)
        if slot == 0:
            locals_[1] = call(
                states_kernel, False,
                where + [("tok", cum), ("tok", step), (("tok", span, 1), x), ("tok", b), (("all", span, 1), oh)],
                own_outs, [(STATE, span), (1, span)], "states",
            )
            diagonal(where, 0)
            return locals_[1]
        if slot == 1:
            diagonal(where, 1)
        if slot == -1:
            sin[0] = arrived
            stats = output(where, 0)

    _, sin[1] = relay(locals_[0][0], locals_[0][1], "seq", True, forward_work)
    plain = [("smem", lengths), ("smem", offset)]
    stats = output(plain, 1)
    exchange = partial(lax.ppermute, axis_name="head", perm=[(0, 1), (1, 0)])
    other = exchange(stats)
    total_width = float(width * lax.axis_size("head"))
    norms = [None, None]

    def norm(where, h):
        kernel = partial(norm_kernel, total_width=total_width)
        ins = where + [("tok", stats), ("tok", other), ("tok", cum), ("tok", step)]
        ins = ins + [(("tok", span, h), v) for v in (x, z, grad)]
        ins = ins + [("tok", b), ("tok", c), ("tok", yp[h]), ("all", dskip), (("all", span, h), gain), (("all", span, h), oh), ("blk", locals_[h][3])]
        aliases = {}
        if h:
            aliases = {len(ins): 0, len(ins) + 1: 1}
            ins = ins + [("any", v) for v in norms[0][:2]]
        else:
            inner = kernel
            kernel = lambda *refs: inner(*refs[:16], None, None, *refs[16:])
        norms[h] = call(
            kernel, True, ins,
            [(("tok", span, h), wide, BF16), (("tok", span, h), wide, BF16), ("tok", half, BF16), ("tok", half, BF16),
             ("all", (1, span), F32), ("blk", states, F32), ("all", (HALF_CHUNKS, STATE, chunk), F32)],
            [(STATE, span)], "norm", aliases,
        )

    norm(plain, 0)
    xparts, carry, partly = [], [], []

    def back(where, q):
        h, sub = q // 2, q % 2
        _, _, ends, _, prefix = locals_[h]
        _, _, dyh, dyl = norms[h][:4]
        out = call(
            partial(diagonal_back_kernel, part=q, last=q == 3), False,
            where + [("tok", cum), ("row", rows), ("tok", step), (("tok", quarter, q), x), ("tok", b), ("tok", c)]
            + [(("tok", quarter, sub), v) for v in (dyh, dyl, yp[h])]
            + [(("all", quarter, sub), sin[h]), (("prev", quarter, sub), ends), (("prev", quarter, sub), prefix), (("all", quarter, q), oh), ("all", dskip)]
            + [("tok", value) for value in carry],
            [("tok", (tokens, quarter), F32)] + [("tok", narrow, F32)] * 5, [], "diagonal_back",
        )
        xparts.append(out[0])
        carry[:] = out[1:]

    def entry(where, h, sout, more):
        _, _, ends, decs, prefix = locals_[h]
        return where + [("all", sout), ("all", sin[h]), ("blk", norms[h][5]), ("blk", decs), ("blk", ends), ("blk", prefix), ("tok", cum),
                        ("tok", step), (("tok", span, h), x), ("tok", b), ("tok", xparts[2 * h]), ("tok", xparts[2 * h + 1]),
                        (("all", span, h), oh)] + more

    def backward_work(slot, message, arrived):
        where = tied(message)
        if slot == 0:
            norm(where, 1)
            back(where, 0)
            return norms[1][6], locals_[1][1]
        if slot == -1:
            back(where, 3)
            partly[:] = call(
                partial(input_kernel, final=False), True, entry(where, 0, arrived, []),
                [(("tok", span, 0), wide, BF16), ("tok", narrow, F32), ("tok", narrow, F32), ("blk", (blocks, 8, LANES), F32)],
                [(STATE, span), (1, span)], "input",
            )
            return
        back(where, slot)

    _, sout = relay(norms[0][6], locals_[0][1], "seq", False, backward_work)
    dbd, dc, rho1, rho2, rho3 = carry
    dc_other = exchange(dc)
    members = lax.axis_size(("seq", "batch"))
    ins = entry(plain, 1, sout, [
        ("any", partly[0]), ("tok", partly[1]), ("tok", partly[2]), ("blk", partly[3]), ("tok", c), ("tok", rho1), ("tok", rho2), ("tok", rho3),
        ("tok", sig), ("all", alog), ("tok", dbd), ("tok", dc), ("tok", dc_other), ("all", norms[0][4]), ("all", norms[1][4]),
    ])
    xgrad, db, dc, draw, sums = call(
        partial(input_kernel, final=True), True, ins,
        [(("tok", span, 1), wide, BF16), ("tok", narrow, F32), ("tok", narrow, F32), ("raw", (heads, tokens), F32),
         ("all", (members, 8 + width // LANES, LANES), F32)],
        [(STATE, span), (1, span), (8, LANES)], "input_last", {15: 0},
    )
    db = db + exchange(db)
    sums = jnp.sum(lax.all_to_all(sums, ("seq", "batch"), 0, 0), axis=0)
    return (
        norms[1][0][None],
        xgrad[None],
        norms[1][1][None],
        db[None],
        dc[None],
        draw.T[None],
        sums[0, :heads],
        sums[1, :heads],
        sums[2, :heads],
        sums[8:].reshape(width),
    )


def solution(mesh):
    wide = P(("groups", "batch"), "seq", "head")
    shared = P(("groups", "batch"), "seq", None)
    part = P(("groups", "head"))
    head = P("head")
    return jax.shard_map(
        shards,
        mesh=mesh,
        in_specs=(wide, wide, shared, shared, wide, P(("groups", "batch"), None), head, head, head, head, wide),
        out_specs=(wide, wide, wide, shared, shared, wide, part, part, part, part),
        check_vma=False,
    )
```

```python
from functools import partial

import jax
import jax.numpy as jnp
import numpy as np
from jax import lax
from jax.experimental import pallas as pl
from jax.experimental.pallas import tpu as pltpu
from jax.sharding import PartitionSpec as P

STATE = 128
HEADDIM = 64
BLOCK = 128
LANES = 128
GROUP = 32
COLS = 256
HALF_CHUNKS = 2
LAG = 2
EPSILON = 1e-05
HIGHEST = lax.Precision.HIGHEST
F32 = jnp.float32
BF16 = jnp.bfloat16
VMEM_LIMIT = 20 * 1024 * 1024


def mm(a, b):
    return jnp.dot(a, b, preferred_element_type=F32)


def mm_nt(a, b):
    return lax.dot_general(a, b, (((1,), (1,)), ((), ())), preferred_element_type=F32)


def mm_tn(a, b):
    return lax.dot_general(a, b, (((0,), (0,)), ((), ())), preferred_element_type=F32)


def split(value):
    high = value.astype(BF16)
    return high, (value - high.astype(F32)).astype(BF16)


def iota(shape, axis):
    return lax.broadcasted_iota(jnp.int32, shape, axis)


def pieces(value):
    high = value.astype(BF16).astype(F32)
    rest = value - high
    middle = rest.astype(BF16).astype(F32)
    lane = iota(value.shape, 1)
    chosen = jnp.where(lane < GROUP, high, jnp.where(lane < 2 * GROUP, middle, rest - middle))
    return jnp.where(lane < 3 * GROUP, chosen, 0.0).astype(BF16)


def head_rows(spread, heads):
    tile = (iota((heads, LANES), 1) % GROUP == iota((heads, LANES), 0)).astype(F32)
    return jnp.dot(jnp.broadcast_to(spread, (8, heads)), tile, precision=HIGHEST, preferred_element_type=F32)[0:1]


def count_starts(lengths, position):
    start = jnp.int32(0)
    total = (start <= position).astype(jnp.int32)
    for k in range(1, lengths.shape[0]):
        start = start + lengths[k - 1]
        total = total + (start <= position).astype(jnp.int32)
    return total


def segments(lengths, offset, block):
    base = offset[0] + block * BLOCK
    column = count_starts(lengths, base + iota((BLOCK, 1), 0))
    row = count_starts(lengths, base + iota((1, BLOCK), 1))
    return column, row, count_starts(lengths, base - 1), count_starts(lengths, base + BLOCK - 1)


def local_states(weights, decays, x, b, oh, e, total, ends, decs, prefix, state, run):
    for at in range(0, x.shape[1], COLS):
        col = slice(at, at + COLS)
        high, low = split(x[:, col].astype(F32) * mm(weights, oh[:, col]))
        dec = mm(decays, oh[:, col])[0:1]
        fresh = dec * state[:, col] + (mm_tn(b[...], high) + mm_tn(b[...], low))
        state[:, col] = fresh
        ends[0, :, col] = fresh
        decs[0, :, col] = dec
        product = run[:, col] * dec
        run[:, col] = product
        prefix[0, :, col] = product

    @pl.when(pl.program_id(0) == pl.num_programs(0) - 1)
    def _():
        chunk = e.shape[2]
        for k in range(e.shape[0]):
            e[k] = state[:, k * chunk : (k + 1) * chunk]
            total[k] = run[:, k * chunk : (k + 1) * chunk]


def clear_states(state, run):
    @pl.when(pl.program_id(0) == 0)
    def _():
        state[...] = jnp.zeros_like(state)
        run[...] = jnp.ones_like(run)


def weigh(cumul, steps, segment, prior, last):
    closing = cumul[BLOCK - 1 : BLOCK, :]
    weight = jnp.exp(closing - cumul) * (segment == last).astype(F32) * steps
    decay = jnp.exp(closing) * (last == prior).astype(F32)
    return pieces(weight), pieces(jnp.broadcast_to(decay, (8, LANES)))


def prepare_kernel(lengths, offset, raw, bias, alog, x, b, oh, e, total, ends, decs, prefix, step, cum, sig, rows, state, run):
    heads = raw.shape[0]
    clear_states(state, run)
    segment, _, prior, last = segments(lengths, offset, pl.program_id(0))
    same = iota((heads, heads), 0) == iota((heads, heads), 1)
    shift = jnp.sum(jnp.where(same, jnp.broadcast_to(bias[...], (heads, heads)), 0.0), axis=1, keepdims=True)
    value = raw[...] + shift
    small = jnp.exp(-jnp.abs(value))
    ratio = small / (2.0 + small)
    square = ratio * ratio
    series = jnp.full_like(square, 1.0 / 19.0)
    for odd in (17, 15, 13, 11, 9, 7, 5, 3, 1):
        series = series * square + 1.0 / odd
    soft = jnp.maximum(value, 0.0) + 2.0 * ratio * series
    inverse = 1.0 / (1.0 + small)
    sigma = jnp.where(value >= 0.0, inverse, small * inverse)
    tile = (iota((heads, LANES), 1) % GROUP == iota((heads, LANES), 0)).astype(F32)
    spread = partial(lax.dot_general, dimension_numbers=(((0,), (0,)), ((), ())), precision=HIGHEST, preferred_element_type=F32)
    steps = spread(soft, tile)
    rate = steps * -jnp.exp(head_rows(alog[...], heads))
    lower = (iota((BLOCK, BLOCK), 0) >= iota((BLOCK, BLOCK), 1)).astype(F32)
    cumul = jnp.dot(lower, rate, precision=HIGHEST, preferred_element_type=F32)
    step[...] = steps
    cum[...] = cumul
    sig[...] = spread(sigma, tile)
    rows[0] = cumul.T[:GROUP]
    rows[1] = steps.T[:GROUP]
    weights, decays = weigh(cumul, steps, segment, prior, last)
    local_states(weights, decays, x, b, oh, e, total, ends, decs, prefix, state, run)


def states_kernel(lengths, offset, cum, step, x, b, oh, e, total, ends, decs, prefix, state, run):
    clear_states(state, run)
    segment, _, prior, last = segments(lengths, offset, pl.program_id(0))
    weights, decays = weigh(cum[...], step[...], segment, prior, last)
    local_states(weights, decays, x, b, oh, e, total, ends, decs, prefix, state, run)


def diagonal_kernel(lengths, offset, cum, rows, x, b, c, out, *, first):
    block = pl.program_id(0)
    seg_column, seg_row, _, _ = segments(lengths, offset, block)
    mask = (seg_column == seg_row) & (iota((BLOCK, BLOCK), 0) > iota((BLOCK, BLOCK), 1))
    scores = jnp.where(mask, mm_nt(c[...], b[...]), 0.0)
    left = iota((BLOCK, LANES), 1) < HEADDIM
    for pair in range(x.shape[1] // LANES):
        col = slice(pair * LANES, (pair + 1) * LANES)
        parts = []
        for h in (first + 2 * pair, first + 2 * pair + 1):
            gap = cum[:, h : h + 1] - rows[0, h : h + 1, :]
            parts.append(split(jnp.exp(jnp.minimum(gap, 0.0)) * scores * rows[1, h : h + 1, :]))
        pair_x = x[:, col]
        zero = jnp.zeros_like(pair_x)
        both = jnp.concatenate([jnp.where(left, pair_x, zero), jnp.where(left, zero, pair_x)], axis=0)
        high = jnp.concatenate([parts[0][0], parts[1][0]], axis=1)
        low = jnp.concatenate([parts[0][1], parts[1][1]], axis=1)
        out[:, col] = mm(high, both) + mm(low, both)


def output_kernel(lengths, offset, sin, ends, prefix, cum, step, x, z, g, b, c, diag, dskip, gain, oh, before, yp, stats, state):
    block = pl.program_id(0)

    @pl.when(block == 0)
    def _():
        state[...] = sin[...]

    segment, _, prior, _ = segments(lengths, offset, block)
    inflow = pieces(jnp.exp(cum[...]) * (segment == prior).astype(F32))
    own = jnp.sum(b[...].astype(F32) * c[...].astype(F32), axis=1, keepdims=True)
    coefficient = pieces(head_rows(dskip[...], dskip.shape[1]) + step[...] * own)
    square = jnp.zeros((BLOCK, COLS), F32)
    cross = jnp.zeros((BLOCK, COLS), F32)
    for at in range(0, x.shape[1], COLS):
        col = slice(at, at + COLS)
        high, low = split(state[:, col])
        carried = mm(c[...], high) + mm(c[...], low)
        partial_out = mm(inflow, oh[:, col]) * carried + diag[:, col]
        yp[:, col] = partial_out
        y = partial_out + mm(coefficient, oh[:, col]) * x[:, col].astype(F32)
        zf = z[:, col].astype(F32)
        gated = y * (zf / (1.0 + jnp.exp(-zf)))
        square = square + gated * gated
        cross = cross + g[:, col].astype(F32) * gain[:, col] * gated
        state[:, col] = ends[0, :, col] + prefix[0, :, col] * sin[:, col]
    lane = iota((BLOCK, LANES), 1)
    sums = jnp.where(lane == 0, jnp.sum(square, axis=1, keepdims=True), 0.0)
    sums = sums + jnp.where(lane == 1, jnp.sum(cross, axis=1, keepdims=True), 0.0)
    stats[...] = sums if before is None else before[...] + sums


def norm_kernel(lengths, offset, mine, other, cum, step, x, z, g, b, c, yp, dskip, gain, oh, decs, _n, _z, normed, zgrad, dyh, dyl, gpart, starts, own_grad, state, *, total_width):
    turn = pl.program_id(0)
    block = pl.num_programs(0) - 1 - turn

    @pl.when(turn == 0)
    def _():
        state[...] = jnp.zeros_like(state)
        gpart[...] = jnp.zeros_like(gpart)

    segment, _, prior, _ = segments(lengths, offset, block)
    inflow = pieces(jnp.exp(cum[...]) * (segment == prior).astype(F32))
    own = jnp.sum(b[...].astype(F32) * c[...].astype(F32), axis=1, keepdims=True)
    coefficient = pieces(head_rows(dskip[...], dskip.shape[1]) + step[...] * own)
    both = mine[...] + other[...]
    mean = both[:, 0:1] / total_width + EPSILON
    scale = lax.rsqrt(mean)
    scale = scale * (1.5 - 0.5 * mean * scale * scale)
    factor = scale * scale * scale * (both[:, 1:2] / total_width)
    for at in range(0, x.shape[1], COLS):
        col = slice(at, at + COLS)
        xf = x[:, col].astype(F32)
        y = yp[:, col] + mm(coefficient, oh[:, col]) * xf
        zf = z[:, col].astype(F32)
        sigma = 1.0 / (1.0 + jnp.exp(-zf))
        gate = zf * sigma
        gated = y * gate
        scaled = gated * scale
        gf = g[:, col].astype(F32)
        normed[:, col] = (scaled * gain[:, col]).astype(BF16)
        gpart[:, col] += jnp.sum(gf * scaled, axis=0, keepdims=True)
        grad = gf * gain[:, col] * scale - gated * factor
        zgrad[:, col] = (grad * y * (sigma + gate * (1.0 - sigma))).astype(BF16)
        dy = grad * gate
        high, low = split(dy)
        dyh[:, col] = high
        dyl[:, col] = low
        high, low = split(dy * mm(inflow, oh[:, col]))
        back = decs[0, :, col] * state[:, col] + (mm_tn(c[...], high) + mm_tn(c[...], low))
        state[:, col] = back
        starts[0, :, col] = back

    @pl.when(turn == pl.num_programs(0) - 1)
    def _():
        chunk = own_grad.shape[2]
        for k in range(own_grad.shape[0]):
            own_grad[k] = state[:, k * chunk : (k + 1) * chunk]


def diagonal_back_kernel(lengths, offset, cum, rows, step, x, b, c, dyh, dyl, yp, sin, ends, prefix, oh, dskip, *rest, part, last):
    count = 5 if part else 0
    before, xpart, after = rest[:count], rest[count], rest[count + 1 :]
    block = pl.program_id(0)
    seg_column, seg_row, prior, _ = segments(lengths, offset, block)
    mask = (seg_column == seg_row) & (iota((BLOCK, BLOCK), 1) > iota((BLOCK, BLOCK), 0))
    scores = mm_nt(b[...], c[...])
    left = iota((BLOCK, LANES), 1) < HEADDIM
    sums = [value[...] for value in before] if part else [jnp.zeros((BLOCK, LANES), F32)] * 5
    score_grad, carried_c, rho1, rho2, rho3 = sums
    own_score = jnp.sum(b[...].astype(F32) * c[...].astype(F32), axis=1, keepdims=True)
    coefficient = pieces(head_rows(dskip[...], dskip.shape[1]) + step[...] * own_score)
    step_pieces = pieces(step[...])
    du_pairs = []
    inflow = pieces(jnp.exp(cum[...]) * (seg_column == prior).astype(F32))
    pairs = x.shape[1] // LANES
    for pair in range(pairs):
        col = slice(pair * LANES, (pair + 1) * LANES)
        pair_x, high_dy, low_dy = x[:, col], dyh[:, col], dyl[:, col]
        zero = jnp.zeros_like(pair_x)
        top = jnp.concatenate([jnp.where(left, high_dy, zero), jnp.where(left, low_dy, zero)], axis=1)
        bottom = jnp.concatenate([jnp.where(left, zero, high_dy), jnp.where(left, zero, low_dy)], axis=1)
        both = jnp.concatenate([top, bottom], axis=0)
        products = mm_nt(jnp.concatenate([pair_x, pair_x], axis=1), both)
        parts = []
        for e in (0, 1):
            h = 2 * (part * pairs + pair) + e
            gap = rows[0, h : h + 1, :] - cum[:, h : h + 1]
            decay = jnp.where(mask, jnp.exp(jnp.minimum(gap, 0.0)), 0.0)
            score_grad = score_grad + decay * products[:, e * BLOCK : (e + 1) * BLOCK] * step[:, h : h + 1]
            parts.append(split(decay * scores))
        high = mm(jnp.concatenate([parts[0][0], parts[1][0]], axis=1), both)
        low = mm(jnp.concatenate([parts[0][1], parts[1][1]], axis=1), both[:, :LANES])
        du_pairs.append(high[:, :LANES] + (high[:, LANES:] + low))
    dy = dyh[...].astype(F32) + dyl[...].astype(F32)
    du = jnp.concatenate(du_pairs, axis=1)
    xf = x[...].astype(F32)
    high, low = split(dy * mm(inflow, oh[...]))
    entering = jnp.where(block == 0, sin[...], ends[0] + prefix[0] * sin[...])
    s_high, s_low = split(entering)
    carried_c = carried_c + (mm_nt(high, s_high) + (mm_nt(low, s_high) + mm_nt(high, s_low)))
    xpart[...] = mm(step_pieces, oh[...]) * du + mm(coefficient, oh[...]) * dy
    high, low = split(dy * yp[...])
    rho1 = rho1 + (mm_nt(high, oh[...]) + mm_nt(low, oh[...]))
    high, low = split(xf * du)
    rho2 = rho2 + (mm_nt(high, oh[...]) + mm_nt(low, oh[...]))
    high, low = split(dy * xf)
    rho3 = rho3 + (mm_nt(high, oh[...]) + mm_nt(low, oh[...]))
    if last:
        lane = iota((BLOCK, LANES), 1)
        own = jnp.sum(jnp.where(lane < GROUP, rho3 * step[...], 0.0), axis=1, keepdims=True)
        high, low = split(score_grad)
        score_grad = mm(high, c[...]) + mm(low, c[...]) + own * c[...].astype(F32)
        carried_c = carried_c + (mm_tn(high, b[...]) + mm_tn(low, b[...])) + own * b[...].astype(F32)
    for ref, value in zip(after, (score_grad, carried_c, rho1, rho2, rho3)):
        ref[...] = value


def input_kernel(lengths, offset, sout, sin, starts, decs, ends, prefix, cum, step, x, b, part0, part1, oh, *rest, final):
    if final:
        _, db_in, scaled_in, inner_in, c, rho1, rho2, rho3, sig, alog, dbd, dc_mine, dc_other, gpart0, gpart1 = rest[:15]
        xgrad, db, dc, draw, sums, state, run, small = rest[15:]
    else:
        xgrad, db, scaled_out, inner_out, state, run = rest
    turn = pl.program_id(0)
    block = pl.num_programs(0) - 1 - turn

    @pl.when(turn == 0)
    def _():
        state[...] = sout[...]
        run[...] = jnp.ones_like(run)
        if final:
            small[...] = jnp.zeros_like(small)

    segment, _, prior, last = segments(lengths, offset, block)
    steps = step[...]
    weights, _ = weigh(cum[...], steps, segment, prior, last)
    scaled = scaled_in[...] if final else jnp.zeros((BLOCK, LANES), F32)
    carried_b = db_in[...] if final else jnp.zeros((BLOCK, STATE), F32)
    inner = inner_in[0] if final else jnp.zeros((8, LANES), F32)
    span = part0.shape[1]
    for at, part in ((0, part0), (span, part1)):
        col = slice(at, at + span)
        leaving = state[:, col]
        s_high, s_low = split(leaving)
        wide = mm(weights, oh[:, col])
        xf = x[:, col].astype(F32)
        du = wide * (mm(b[...], s_high) + mm(b[...], s_low))
        xgrad[:, col] = (part[...] + du).astype(BF16)
        high, low = split(xf * du)
        scaled = scaled + (mm_nt(high, oh[:, col]) + mm_nt(low, oh[:, col]))
        high, low = split(xf * wide)
        carried_b = carried_b + (mm_nt(high, s_high) + (mm_nt(low, s_high) + mm_nt(high, s_low)))
        whole = ends[0, :, col] + prefix[0, :, col] * sin[:, col]
        overlap = jnp.sum((whole * leaving).reshape(STATE // 8, 8, span), axis=0)
        high, low = split(overlap)
        inner = inner + (mm_nt(high, oh[:, col]) + mm_nt(low, oh[:, col]))
        product = run[:, col] * decs[0, :, col]
        run[:, col] = product
        state[:, col] = starts[0, :, col] + product * sout[:, col]
    if not final:
        db[...] = carried_b
        scaled_out[...] = scaled
        inner_out[0] = inner
        return
    db[...] = dbd[...] + carried_b
    dc[...] = dc_mine[...] + dc_other[...]
    own = jnp.sum(b[...].astype(F32) * c[...].astype(F32), axis=1, keepdims=True)
    second = rho2[...] + jnp.where(steps > 0.0, scaled / steps, 0.0)
    upper = (iota((BLOCK, BLOCK), 1) >= iota((BLOCK, BLOCK), 0)).astype(F32)
    rate_grad = jnp.dot(upper, rho1[...] - steps * rho2[...] - scaled, precision=HIGHEST, preferred_element_type=F32)
    rate_grad = rate_grad + jnp.sum(inner, axis=0, keepdims=True)
    speed = jnp.exp(head_rows(alog[...], alog.shape[1]))
    raw_grad = (second + own * rho3[...] - speed * rate_grad) * sig[...]
    draw[...] = raw_grad.T[: draw.shape[0]]
    row = iota((8, LANES), 0)
    bias_row = jnp.where(row == 0, jnp.sum(raw_grad, axis=0, keepdims=True), 0.0)
    alog_row = jnp.where(row == 1, jnp.sum(rate_grad * steps * -speed, axis=0, keepdims=True), 0.0)
    skip_row = jnp.where(row == 2, jnp.sum(rho3[...], axis=0, keepdims=True), 0.0)
    small[...] += bias_row + alog_row + skip_row

    @pl.when(turn == pl.num_programs(0) - 1)
    def _():
        rows = gpart0.shape[1] // LANES
        for k in range(sums.shape[0]):
            sums[k, :8] = small[...]
            for r in range(rows):
                sums[k, 8 + r : 9 + r] = gpart0[:, r * LANES : (r + 1) * LANES]
                sums[k, 8 + rows + r : 9 + rows + r] = gpart1[:, r * LANES : (r + 1) * LANES]


def take(array, at):
    start = (at,) + (0,) * (array.ndim - 1)
    return lax.dynamic_slice(array, start, (1,) + array.shape[1:], allow_negative_indices=False)[0]


def relay_steps(count):
    return 2 * HALF_CHUNKS + LAG * (count - 2)


def relay_plan(rank, count):
    chunks, steps = 2 * HALF_CHUNKS, relay_steps(count)
    sends = []
    for turn in range(LAG, steps):
        at = jnp.clip(turn - LAG * rank, 0, chunks - 1)
        sends.append((at < HALF_CHUNKS, [jnp.clip(at - k * HALF_CHUNKS, 0, HALF_CHUNKS - 1) for k in range(2)]))
    arrivals = []
    for which, turns in ((0, steps - LAG), (1, steps)):
        at = [k + which * HALF_CHUNKS + LAG * (rank - 1) for k in range(HALF_CHUNKS)]
        arrivals.append([jnp.clip(k, 0, turns - 1) for k in at])
    return sends, arrivals, rank > 0


def relay(own, total, axis, forward, plan, work):
    count = lax.axis_size(axis)
    chunks, steps = 2 * HALF_CHUNKS, relay_steps(count)
    sends, arrivals, follows = plan
    received, halves, message = [], None, None

    def half(which):
        stacked = jnp.stack(received[: steps - LAG] if which == 0 else received)
        picked = [take(stacked, at) for at in arrivals[which]]
        return jnp.where(follows, jnp.concatenate(picked, axis=1), 0.0)

    for turn in range(steps):
        if turn < LAG:
            mine = own[turn]
            if message is not None:
                mine, _ = lax.optimization_barrier((mine, message))
        else:
            low, at = sends[turn - LAG]
            arrived, _ = lax.optimization_barrier((received[turn - LAG], message))
            mine, factor = (jnp.where(low, take(pair[0], at[0]), take(pair[1], at[1])) for pair in halves)
            mine = mine + factor * arrived
        message = mine
        ranks = [r for r in range(count - 1) if 0 <= turn - LAG * r < chunks]
        pairs = [(r, r + 1) if forward else (count - 1 - r, count - 2 - r) for r in ranks]
        received.append(lax.ppermute(message, axis, pairs))
        if turn == LAG - 1:
            second = work(0, message, None)
            halves = (own, second[0]), (total, second[1])
        elif turn == steps - 1:
            first = half(0)
            work(-1, message, first)
        elif turn % LAG == LAG - 1 and turn < 6:
            work(turn // LAG, message, None)
    return first, half(1)


def placed(kind, shape, dtype):
    return pltpu.VMEM(shape, dtype) if kind in ("tok", "blk", "row") else jax.ShapeDtypeStruct(shape, dtype)


def one_hot(width):
    lane = np.arange(LANES)[:, None]
    return np.logical_and(lane % GROUP == np.arange(width)[None, :] // HEADDIM, lane < 3 * GROUP)


def shards(x, z, b, c, raw, lengths, bias, alog, dskip, gain, grad):
    _, tokens, width = x.shape
    heads = width // HEADDIM
    blocks = tokens // BLOCK
    span, quarter = width // 2, width // 4
    chunk = span // HALF_CHUNKS
    x, z, grad = (v.reshape(tokens, width) for v in (x, z, grad))
    b, c = b.reshape(tokens, STATE), c.reshape(tokens, STATE)
    raw = raw.reshape(tokens, heads).T
    lengths = lengths.reshape(-1)
    bias, alog, dskip = (v.reshape(1, heads) for v in (bias, alog, dskip))
    gain = gain.reshape(1, width)
    oh = jnp.asarray(one_hot(width), BF16)
    x, z, grad, b, c, raw, bias, alog, dskip, gain, oh = (
        pltpu.with_memory_space_constraint(v, pltpu.HBM) for v in (x, z, grad, b, c, raw, bias, alog, dskip, gain, oh)
    )
    count, index = lax.axis_size("seq"), lax.axis_index("seq")
    offset = jnp.reshape(index * tokens, (1,)).astype(jnp.int32)
    plans = relay_plan(index, count), relay_plan(count - 1 - index, count)
    offset, plans = lax.optimization_barrier((offset, plans))

    def tied(message):
        return [("smem", lengths), ("smem", lax.optimization_barrier((offset, message))[0])]

    def call(kernel, reverse, ins, outs, scratch, name, aliases=None):
        place = (lambda i: blocks - 1 - i) if reverse else (lambda i: i)

        def spec(kind, shape):
            kind, step, at = kind if isinstance(kind, tuple) else (kind, shape[-1], 0)
            if kind == "smem":
                return pl.BlockSpec(memory_space=pltpu.SMEM)
            if kind == "any":
                return pl.BlockSpec(memory_space=pl.ANY)
            if kind == "tok":
                return pl.BlockSpec((BLOCK, step), lambda i: (place(i), at))
            if kind == "blk":
                return pl.BlockSpec((1, shape[1], step), lambda i: (place(i), 0, at))
            if kind == "prev":
                return pl.BlockSpec((1, shape[1], step), lambda i: (jnp.maximum(place(i) - 1, 0), 0, at))
            if kind == "raw":
                return pl.BlockSpec((shape[0], BLOCK), lambda i: (0, place(i)))
            if kind == "row":
                return pl.BlockSpec((2, GROUP, BLOCK), lambda i: (0, 0, place(i)))
            return pl.BlockSpec(tuple(shape[:-1]) + (step,), lambda i: (0,) * (len(shape) - 1) + (at,))

        return pl.pallas_call(
            kernel,
            grid=(blocks,),
            in_specs=[spec(kind, value.shape) for kind, value in ins],
            out_specs=[spec(kind, shape) for kind, shape, _ in outs],
            out_shape=[placed(kind, shape, dtype) for kind, shape, dtype in outs],
            scratch_shapes=[pltpu.VMEM(shape, F32) for shape in scratch],
            input_output_aliases=aliases or {},
            compiler_params=pltpu.CompilerParams(
                dimension_semantics=("arbitrary",), vmem_limit_bytes=VMEM_LIMIT
            ),
            name=name,
        )(*[value for _, value in ins])

    wide = (tokens, width)
    half = (tokens, span)
    narrow = (tokens, LANES)
    states = (blocks, STATE, span)
    line = (blocks, 1, span)
    own_outs = [("all", (HALF_CHUNKS, STATE, chunk), F32), ("all", (HALF_CHUNKS, 1, chunk), F32), ("blk", states, F32),
                ("blk", line, F32), ("blk", line, F32)]
    first = call(
        prepare_kernel, False,
        [("smem", lengths), ("smem", offset), ("raw", raw), ("all", bias), ("all", alog), (("tok", span, 0), x), ("tok", b), (("all", span, 0), oh)],
        own_outs + [("tok", narrow, F32), ("tok", narrow, F32), ("tok", narrow, F32), ("row", (2, GROUP, tokens), F32)],
        [(STATE, span), (1, span)], "prepare",
    )
    step, cum, sig, rows = first[5:]
    locals_ = [first[:5], None]
    diag, sin, yp, stats = [None, None], [None, None], [None, None], None

    def diagonal(where, h):
        (diag[h],) = call(
            partial(diagonal_kernel, first=h * heads // 2), False,
            where + [("tok", cum), ("row", rows), (("tok", span, h), x), ("tok", b), ("tok", c)],
            [("tok", half, F32)], [], "diagonal",
        )

    def output(where, h):
        kernel = output_kernel if h else (lambda *refs: output_kernel(*refs[:16], None, *refs[16:]))
        _, _, ends, _, prefix = locals_[h]
        yp[h], total = call(
            kernel, False,
            where + [("all", sin[h]), ("blk", ends), ("blk", prefix), ("tok", cum), ("tok", step)]
            + [(("tok", span, h), v) for v in (x, z, grad)]
            + [("tok", b), ("tok", c), ("tok", diag[h]), ("all", dskip), (("all", span, h), gain), (("all", span, h), oh)]
            + ([("tok", stats)] if h else []),
            [("tok", half, F32), ("tok", narrow, F32)], [(STATE, span)], "output",
        )
        return total

    def forward_work(slot, message, arrived):
        nonlocal stats
        where = tied(message)
        if slot == 0:
            locals_[1] = call(
                states_kernel, False,
                where + [("tok", cum), ("tok", step), (("tok", span, 1), x), ("tok", b), (("all", span, 1), oh)],
                own_outs, [(STATE, span), (1, span)], "states",
            )
            diagonal(where, 0)
            return locals_[1]
        if slot == 1:
            diagonal(where, 1)
        if slot == -1:
            sin[0] = arrived
            stats = output(where, 0)

    _, sin[1] = relay(locals_[0][0], locals_[0][1], "seq", True, plans[0], forward_work)
    plain = [("smem", lengths), ("smem", offset)]
    stats = output(plain, 1)
    exchange = partial(lax.ppermute, axis_name="head", perm=[(0, 1), (1, 0)])
    other = exchange(stats)
    total_width = float(width * lax.axis_size("head"))
    norms = [None, None]

    def norm(where, h):
        kernel = partial(norm_kernel, total_width=total_width)
        ins = where + [("tok", stats), ("tok", other), ("tok", cum), ("tok", step)]
        ins = ins + [(("tok", span, h), v) for v in (x, z, grad)]
        ins = ins + [("tok", b), ("tok", c), ("tok", yp[h]), ("all", dskip), (("all", span, h), gain), (("all", span, h), oh), ("blk", locals_[h][3])]
        aliases = {}
        if h:
            aliases = {len(ins): 0, len(ins) + 1: 1}
            ins = ins + [("any", v) for v in norms[0][:2]]
        else:
            inner = kernel
            kernel = lambda *refs: inner(*refs[:16], None, None, *refs[16:])
        norms[h] = call(
            kernel, True, ins,
            [(("tok", span, h), wide, BF16), (("tok", span, h), wide, BF16), ("tok", half, BF16), ("tok", half, BF16),
             ("all", (1, span), F32), ("blk", states, F32), ("all", (HALF_CHUNKS, STATE, chunk), F32)],
            [(STATE, span)], "norm", aliases,
        )

    norm(plain, 0)
    xparts, carry, partly = [], [], []

    def back(where, q):
        h, sub = q // 2, q % 2
        _, _, ends, _, prefix = locals_[h]
        _, _, dyh, dyl = norms[h][:4]
        out = call(
            partial(diagonal_back_kernel, part=q, last=q == 3), False,
            where + [("tok", cum), ("row", rows), ("tok", step), (("tok", quarter, q), x), ("tok", b), ("tok", c)]
            + [(("tok", quarter, sub), v) for v in (dyh, dyl, yp[h])]
            + [(("all", quarter, sub), sin[h]), (("prev", quarter, sub), ends), (("prev", quarter, sub), prefix), (("all", quarter, q), oh), ("all", dskip)]
            + [("tok", value) for value in carry],
            [("tok", (tokens, quarter), F32)] + [("tok", narrow, F32)] * 5, [], "diagonal_back",
        )
        xparts.append(out[0])
        carry[:] = out[1:]

    def entry(where, h, sout, more):
        _, _, ends, decs, prefix = locals_[h]
        return where + [("all", sout), ("all", sin[h]), ("blk", norms[h][5]), ("blk", decs), ("blk", ends), ("blk", prefix), ("tok", cum),
                        ("tok", step), (("tok", span, h), x), ("tok", b), ("tok", xparts[2 * h]), ("tok", xparts[2 * h + 1]),
                        (("all", span, h), oh)] + more

    def backward_work(slot, message, arrived):
        where = tied(message)
        if slot == 0:
            norm(where, 1)
            back(where, 0)
            return norms[1][6], locals_[1][1]
        if slot == -1:
            back(where, 3)
            partly[:] = call(
                partial(input_kernel, final=False), True, entry(where, 0, arrived, []),
                [(("tok", span, 0), wide, BF16), ("tok", narrow, F32), ("tok", narrow, F32), ("blk", (blocks, 8, LANES), F32)],
                [(STATE, span), (1, span)], "input",
            )
            return
        back(where, slot)

    _, sout = relay(norms[0][6], locals_[0][1], "seq", False, plans[1], backward_work)
    dbd, dc, rho1, rho2, rho3 = carry
    dc_other = exchange(dc)
    members = lax.axis_size(("seq", "batch"))
    ins = entry(plain, 1, sout, [
        ("any", partly[0]), ("tok", partly[1]), ("tok", partly[2]), ("blk", partly[3]), ("tok", c), ("tok", rho1), ("tok", rho2), ("tok", rho3),
        ("tok", sig), ("all", alog), ("tok", dbd), ("tok", dc), ("tok", dc_other), ("all", norms[0][4]), ("all", norms[1][4]),
    ])
    xgrad, db, dc, draw, sums = call(
        partial(input_kernel, final=True), True, ins,
        [(("tok", span, 1), wide, BF16), (("tok", LANES, 0), narrow, F32), (("tok", LANES, 0), narrow, F32), ("raw", (heads, tokens), F32),
         ("all", (members, 8 + width // LANES, LANES), F32)],
        [(STATE, span), (1, span), (8, LANES)], "input_last", {15: 0},
    )
    db = db + exchange(db)
    sums = jnp.sum(lax.all_to_all(sums, ("seq", "batch"), 0, 0), axis=0)
    return (
        norms[1][0][None],
        xgrad[None],
        norms[1][1][None],
        db[None],
        dc[None],
        draw.T[None],
        sums[0, :heads],
        sums[1, :heads],
        sums[2, :heads],
        sums[8:].reshape(width),
    )


def solution(mesh):
    wide = P(("groups", "batch"), "seq", "head")
    shared = P(("groups", "batch"), "seq", None)
    part = P(("groups", "head"))
    head = P("head")
    return jax.shard_map(
        shards,
        mesh=mesh,
        in_specs=(wide, wide, shared, shared, wide, P(("groups", "batch"), None), head, head, head, head, wide),
        out_specs=(wide, wide, wide, shared, shared, wide, part, part, part, part),
        check_vma=False,
    )
```
